512 devices in a mesh: lat: 128 (over x, z, core), chan: 4 (over y).
Axes of the slice: x: 4, y: 4, z: 16, core: 2. Of those that a mesh axis runs over, the one named last changes fastest.
Arguments:
- grid: bfloat16 [384, 720, 512], P('lat', None, 'chan'), may hold values from -6 to 6
- basis: float32 [384, 384, 384], P('lat'), may hold values from -16 to 16, as said below
- mix_weight: bfloat16 [2, 512, 512], P(None, None, 'chan'), may hold values from -0.1875 to 0.1875
- spectral_gain: float32 [384], replicated, may hold values from 0.5 to 4
- conv_weight: float32 [9, 512], P(None, 'chan'), may hold values from -2 to 2
- lat_offsets: int32 [9], replicated, may hold values from -1 to 1
- lon_offsets: int32 [9], replicated, may hold values from -3 to 3
- ln_gain: float32 [512], replicated, may hold values from 0.1 to 1.9
- up_weight: bfloat16 [512, 512], replicated, may hold values from -0.25 to 0.25
- down_weight: bfloat16 [512, 512], replicated, may hold values from -0.25 to 0.25
Outputs:
- result: bfloat16 [384, 720, 512], P('lat', None, 'chan')
The draws below stay inside these ranges and needn't reach their ends.
Inputs may be any that keep to these rules, and one draw needn't show every extreme that they name: basis[m, l, t] is the orthonormal associated Legendre function of degree l and order m at cos(theta_t) times a factor between 0.8 and 1.25; it is zero for l < m.
All inputs are finite; a program needn't handle non-finite values.
Results may differ from the reference program's by a relative error of at most 0.01.
Values may be sent and summed in bfloat16 or wider, within the bound.
A program may use at most 64 MiB of HBM per device.

```python
import math
import jax
import jax.numpy as jnp
from jax import lax

NLAT = 384
NLON = 720
C = 512
HID = 512
MMAX = 384
L = 384
NB = 9


def legendre_table(nlat, orders_count, degrees):
    orders = jnp.arange(orders_count, dtype=jnp.int32)
    theta = math.pi * (jnp.arange(nlat, dtype=jnp.int32).astype(jnp.float32) + 0.5) / nlat
    cosine = jnp.cos(theta)[None, :]
    sine = jnp.sin(theta)[None, :]
    order = orders.astype(jnp.float32)[:, None]
    logdiag = 0.5 * (jnp.log(2.0 * order + 1.0) - math.log(2.0) + lax.lgamma(order + 0.5) - 0.5 * math.log(math.pi) - lax.lgamma(order + 1.0))
    diagonal = jnp.exp(logdiag + order * jnp.log(sine))
    start = jnp.zeros((orders_count, nlat), jnp.float32)

    def advance(carry, degree):
        prev_one, prev_two = carry
        level = degree.astype(jnp.float32)
        factor = jnp.sqrt(jnp.maximum(4.0 * level * level - 1.0, 1.0) / jnp.maximum(level * level - order * order, 1.0))
        below = level - 1.0
        inverse_prev = jnp.sqrt(jnp.maximum(below * below - order * order, 1.0) / jnp.maximum(4.0 * below * below - 1.0, 1.0))
        recursed = factor * (cosine * prev_one - prev_two * inverse_prev)
        fresh = jnp.where(level < order, 0.0, jnp.where(level == order, diagonal, recursed))
        return ((fresh, prev_one), fresh)
    _, table = lax.scan(advance, (start, start), jnp.arange(degrees, dtype=jnp.int32))
    return jnp.transpose(table, (1, 0, 2))


def draw_basis(key, part):
    table = legendre_table(NLAT, MMAX, L)
    factor = jax.random.uniform(jax.random.fold_in(key, 17), (MMAX, L, NLAT), jnp.float32, 0.8, 1.25)
    return (table * factor).astype(jnp.float32)


def set_ends(drawn, stream_key, low, high):
    index_at = [jax.random.randint(jax.random.fold_in(stream_key, axis), (), 0, length) for axis, length in enumerate(drawn.shape)]
    longest = drawn.shape.index(max(drawn.shape))
    beside = index_at[:longest] + [(index_at[longest] + 1) % drawn.shape[longest]] + index_at[longest + 1:]
    return drawn.at[tuple(index_at)].set(low).at[tuple(beside)].set(high)


def block_scale(stream_key, dims, shards, low, top_value):
    gain = 1.0
    for axis_at, blocks in shards:
        heights = jax.random.uniform(jax.random.fold_in(jax.random.fold_in(stream_key, 6), axis_at), (blocks,), jnp.float32, low / len(shards), top_value / len(shards))
        gain = gain * jnp.repeat(jnp.exp(heights), dims[axis_at] // blocks).reshape((-1,) + (1,) * (len(dims) - 1 - axis_at))
    return gain


def noise(own_key, extent, width, most, shards=(), kind=jnp.bfloat16):
    values = jax.random.normal(own_key, extent, jnp.float32) * width
    if len(shards) > 0:
        values = block_scale(own_key, extent, shards, -0.22, 0.18) * values
    return jnp.clip(values, min=-most, max=most).astype(kind)


def setup_inputs(seed: int = 0) -> dict:
    key_of = jax.random.split(jax.random.key(seed), 11)
    return {
        "grid": noise(key_of[0], (NLAT, NLON, C), 1.0, 6.0, ((0, 128), (2, 4))),
        "basis": draw_basis(jax.random.fold_in(key_of[10], 71), 0),
        "mix_weight": noise(key_of[2], (2, C, C), (2 * C) ** -0.5, 0.1875, ((2, 4),)),
        "spectral_gain": jnp.clip(jnp.exp(jax.random.uniform(key_of[3], (L,), jnp.float32, math.log(0.5), math.log(4.0))), 0.5, 4.0),
        "conv_weight": noise(key_of[4], (NB, C), NB ** -0.5, 2.0, ((1, 4),), jnp.float32),
        "lat_offsets": set_ends(jax.random.randint(key_of[5], (NB,), -1, 2), jax.random.fold_in(key_of[5], 1), -1, 1).astype(jnp.int32),
        "lon_offsets": set_ends(jax.random.randint(key_of[6], (NB,), -3, 4), jax.random.fold_in(key_of[6], 1), -3, 3).astype(jnp.int32),
        "ln_gain": jnp.clip(1.0 + 0.18 * jax.random.normal(key_of[7], (C,), jnp.float32), 0.1, 1.9),
        "up_weight": noise(key_of[8], (C, HID), C ** -0.5, 0.25),
        "down_weight": noise(key_of[9], (HID, C), HID ** -0.5, 0.25),
    }


def cycle_angle(rows, nlat):
    return math.pi * (rows.astype(jnp.float32) + 0.5) / nlat

def mlp_rows(summed, ln_gain, up_weight, down_weight):
    rows = summed.astype(jnp.float32)
    center = lax.optimization_barrier(jnp.mean(rows, axis=-1, keepdims=True))
    spread = lax.optimization_barrier(jnp.mean((rows - center) ** 2, axis=-1, keepdims=True))
    normed = ((rows - center) / jnp.sqrt(spread + 1e-05) * ln_gain).astype(jnp.bfloat16)
    hidden = jax.nn.gelu(jnp.dot(normed, up_weight, preferred_element_type=jnp.float32), approximate=True).astype(jnp.bfloat16)
    return (jnp.dot(hidden, down_weight, preferred_element_type=jnp.float32) + rows).astype(jnp.bfloat16)

def reference(grid, basis, mix_weight, spectral_gain, conv_weight, lat_offsets, lon_offsets, ln_gain, up_weight, down_weight):
    points = jnp.arange(NLON, dtype=jnp.int32)
    orders = jnp.arange(MMAX, dtype=jnp.int32)
    phase = points[:, None] * orders[None, :] % NLON
    angle = 2.0 * math.pi * phase.astype(jnp.float32) / NLON
    fwd_table = jnp.concatenate([jnp.cos(angle), -jnp.sin(angle)], axis=1).astype(jnp.bfloat16)
    weight_m = jnp.where(orders == 0, 1.0, 2.0).astype(jnp.float32)[None, :]
    inv_table = jnp.concatenate([weight_m * jnp.cos(angle), -weight_m * jnp.sin(angle)], axis=1).astype(jnp.bfloat16)

    def forward_row(row):
        return (jnp.dot(fwd_table.T, row, preferred_element_type=jnp.float32) * (1.0 / NLON)).astype(jnp.bfloat16)
    spec = lax.map(forward_row, grid)
    spec = jnp.transpose(spec.reshape(NLAT, 2, MMAX, C), (2, 0, 1, 3)).reshape(MMAX, NLAT, 2 * C)
    theta = cycle_angle(jnp.arange(NLAT, dtype=jnp.int32), NLAT)
    quad = math.pi / NLAT * jnp.sin(theta)
    fwd_leg = (basis * quad[None, None, :]).astype(jnp.bfloat16)
    inv_leg = basis.astype(jnp.bfloat16)

    def forward_mode(pair):
        return jnp.dot(pair[0], pair[1], preferred_element_type=jnp.float32).astype(jnp.bfloat16)
    coeff = lax.map(forward_mode, (fwd_leg, spec))
    real_part = mix_weight[0]
    imag_part = mix_weight[1]
    block = jnp.concatenate([jnp.concatenate([real_part, imag_part], axis=1), jnp.concatenate([-imag_part, real_part], axis=1)], axis=0)
    mixed = jnp.dot(coeff.reshape(MMAX * L, 2 * C), block, preferred_element_type=jnp.float32).reshape(MMAX, L, 2 * C)
    mixed = (mixed * spectral_gain[None, :, None]).astype(jnp.bfloat16)

    def inverse_mode(pair):
        return jnp.dot(pair[0].T, pair[1], preferred_element_type=jnp.float32).astype(jnp.bfloat16)
    back = lax.map(inverse_mode, (inv_leg, mixed))
    back = jnp.transpose(back.reshape(MMAX, NLAT, 2, C), (1, 2, 0, 3)).reshape(NLAT, 2 * MMAX, C)
    padded = jnp.pad(grid, ((1, 1), (0, 0), (0, 0)))

    def output_row(inputs):
        cycle, back_row, grid_row = inputs
        spectral = jnp.dot(inv_table, back_row, preferred_element_type=jnp.float32)
        local = jnp.zeros((NLON, C), jnp.float32)
        here = jnp.sin(cycle_angle(cycle, NLAT))
        for tap in range(NB):
            shift = lat_offsets[tap]
            source = lax.dynamic_slice_in_dim(padded, (cycle + 1 + shift).astype(jnp.int32), 1, 0)[0]
            source = jnp.roll(source, -lon_offsets[tap], axis=0)
            ratio = jnp.sin(cycle_angle(cycle + shift, NLAT)) / here
            local = local + conv_weight[tap][None, :] * ratio * source.astype(jnp.float32)
        summed = (spectral + local + grid_row.astype(jnp.float32)).astype(jnp.bfloat16)
        return mlp_rows(summed, ln_gain, up_weight, down_weight)
    return lax.map(output_row, (jnp.arange(NLAT, dtype=jnp.int32), back, grid))
```

```python
import functools
import math

import jax
import jax.numpy as jnp
import ml_dtypes
import numpy as np
from jax import lax
from jax.experimental import pallas as pl
from jax.experimental.pallas import tpu as pltpu
from jax.sharding import Mesh
from jax.sharding import PartitionSpec as P

LAT = ("lat_0", "lat_1", "lat_2")
MESH_ID = pl.DeviceIdType.MESH
TILE = 16
F32 = jnp.float32
BF16 = jnp.bfloat16


def transform_tables(X, Z, K, modes, nlon):
    z, ri, x, k, j = np.meshgrid(
        np.arange(Z), np.arange(2), np.arange(X), np.arange(K), np.arange(modes), indexing="ij"
    )
    m = (((x * Z + z) * K + k) * modes + j).reshape(-1).astype(np.int64)
    part = ri.reshape(-1)
    points = np.arange(nlon, dtype=np.int64)
    phase = (m[:, None] * points[None, :]) % nlon
    angle = np.float32(2.0 * math.pi) * phase.astype(np.float32) / np.float32(nlon)
    table = np.where(part[:, None] == 0, np.cos(angle), -np.sin(angle)).astype(np.float32)
    return table.astype(ml_dtypes.bfloat16)


def cycle_order(X, Z, K, cycles):
    c, x, k, z = np.meshgrid(
        np.arange(cycles), np.arange(X), np.arange(K), np.arange(Z), indexing="ij"
    )
    return (((x * Z + z) * K + k) * cycles + c).reshape(-1)


def block_kernel(
    dims,
    grid_in,
    table_in,
    inverse_in,
    perm_in,
    basis_in,
    mix_in,
    gain_in,
    quad_in,
    conv_in,
    lat_off,
    lon_off,
    norm_in,
    up_in,
    down_in,
    out,
    grid_v,
    table,
    inverse,
    perm,
    basis,
    mix_all,
    up_w,
    down_w,
    leg,
    leg_t,
    z1_send,
    z1_recv,
    x1_send,
    x1_recv,
    acc,
    scaled,
    x2_send,
    x2_recv,
    z2_send,
    z2_recv,
    halo,
    padded,
    local_send,
    local_recv,
    field_send,
    field_recv,
    out_send,
    out_recv,
    load_sem,
    send_sem,
    recv_sem,
):
    X, Z, K, Y, cycles, modes, L, nlon, width, step, size = dims
    Q = X * K
    R = Q * Z
    rows = 2 * Q * modes
    half = Q * modes
    x = lax.axis_index("lat_0")
    z = lax.axis_index("lat_1")
    k = lax.axis_index("lat_2")
    y = lax.axis_index("chan")
    q = x * K + k
    rank = (x * Z + z) * K + k

    loads = [
        (table_in, table),
        (grid_in, grid_v),
        (basis_in, basis),
        (perm_in, perm),
        (inverse_in, inverse),
        (up_in, up_w),
        (down_in, down_w),
        (mix_in, mix_all.at[y]),
    ]
    copies = [
        pltpu.make_async_copy(src, dst, load_sem.at[i]) for i, (src, dst) in enumerate(loads)
    ]
    for copy in copies:
        copy.start()

    def z_device(i):
        return {"lat_1": lax.rem(z + i, Z)}

    def q_device(i):
        other = lax.rem(q + i, Q)
        return {"lat_0": other // K, "lat_2": lax.rem(other, K)}

    def y_device(i):
        return {"chan": lax.rem(y + i, Y)}

    def rank_device(r):
        return {"lat_0": r // (Z * K), "lat_1": lax.rem(r // K, Z), "lat_2": lax.rem(r, K)}

    barrier = pltpu.get_barrier_semaphore()

    def greet(device):
        pl.semaphore_signal(barrier, inc=1, device_id=device, device_id_type=MESH_ID)

    @pl.loop(1, Z)
    def _(i):
        greet(z_device(i))

    @pl.loop(1, Q)
    def _(i):
        greet(q_device(i))

    @pl.loop(1, Y)
    def _(i):
        greet(y_device(i))

    @pl.when(rank > 0)
    def _():
        greet(rank_device(rank - 1))

    @pl.when(rank < R - 1)
    def _():
        greet(rank_device(rank + 1))

    def send(src, dst, at, device):
        pltpu.make_async_remote_copy(
            src_ref=src,
            dst_ref=dst,
            send_sem=send_sem.at[at],
            recv_sem=recv_sem.at[at],
            device_id=device,
            device_id_type=MESH_ID,
        ).start()

    def await_recv(ref, at):
        pltpu.make_async_copy(ref, ref, recv_sem.at[at]).wait()

    def await_send(ref, at):
        pltpu.make_async_copy(ref, ref, send_sem.at[at]).wait()

    Z1, X1, X2, Z2, FIELD, OUT = (n * cycles for n in range(6))
    LOCAL = 6 * cycles
    MIX = LOCAL + 1
    BEFORE = LOCAL + 2
    AFTER = LOCAL + 3
    EXTRA = LOCAL + 4

    def forward(c):
        spec = jnp.dot(table[...], grid_v[c], preferred_element_type=F32) * (1.0 / nlon)
        spec = spec.astype(BF16).reshape(Z, rows, width)
        z1_send[c] = spec

    def send_z(buf, land, c, at):
        @pl.loop(0, Z - 1)
        def _(i):
            far = Z - 1 - i
            offset = jnp.where(lax.rem(far, 2) == 1, (far + 1) // 2, Z - far // 2)
            other = lax.rem(z + offset, Z)
            send(buf.at[c, other], land.at[c, z], at + c, {"lat_1": other})

        land[c, z] = buf[c, z]

    def send_q(buf, land, c, at):
        @pl.loop(1, Q)
        def _(i):
            other = lax.rem(q + i, Q)
            device = {"lat_0": other // K, "lat_2": lax.rem(other, K)}
            send(buf.at[c, other], land.at[c, q], at + c, device)

        land[c, q] = buf[c, q]

    copies[0].wait()
    copies[1].wait()
    forward(0)
    greeted = (Z - 1) + (Q - 1) + (Y - 1)
    greeted = greeted + jnp.where(rank > 0, 1, 0) + jnp.where(rank < R - 1, 1, 0)
    pl.semaphore_wait(barrier, greeted)
    send_z(z1_send, z1_recv, 0, Z1)
    for c in range(1, cycles):
        forward(c)
        send_z(z1_send, z1_recv, c, Z1)

    @pl.when(rank < R - 1)
    def _():
        send(grid_v.at[cycles - 1], halo.at[0], BEFORE, rank_device(rank + 1))

    @pl.when(rank > 0)
    def _():
        send(grid_v.at[0], halo.at[1], AFTER, rank_device(rank - 1))

    copies[7].wait()

    @pl.loop(1, Y)
    def _(i):
        send(mix_all.at[y], mix_all.at[y], MIX, y_device(i))

    copies[2].wait()
    copies[3].wait()
    for j in range(modes):
        weighted = (basis[j] * quad_in[...]).astype(BF16)
        leg[j] = lax.dot_general(
            weighted, perm[...], (((1,), (1,)), ((), ())), preferred_element_type=F32
        ).astype(BF16)
        leg_t[j] = lax.dot_general(
            perm[...], basis[j].astype(BF16), (((1,), (1,)), ((), ())), preferred_element_type=F32
        ).astype(BF16)

    def to_wavenumbers(c):
        await_recv(z1_recv.at[c, pl.ds(0, Z - 1)], Z1 + c)
        turned = jnp.swapaxes(z1_recv[c].astype(F32), 0, 1).astype(BF16)
        turned = turned.reshape(2, Q, modes, Z, width)
        for j in range(modes):
            for part in range(2):
                x1_send[c, :, 2 * j + part] = turned[part, :, j]
        send_q(x1_send, x1_recv, c, X1)

    def legendre(c):
        await_recv(x1_recv.at[c, pl.ds(0, Q - 1)], X1 + c)
        for j in range(modes):
            parts = [x1_recv[c, :, 2 * j + part].reshape(Q * Z, width) for part in range(2)]
            values = jnp.concatenate(parts, axis=1)
            found = jnp.dot(
                leg[j, :, c * Q * Z : (c + 1) * Q * Z], values, preferred_element_type=F32
            )
            if c == 0:
                acc[j] = found
            else:
                acc[j] += found

    def local_field():
        pad = (padded.shape[1] - nlon) // 2

        def place(at, values):
            padded[at, pad : pad + nlon] = values
            padded[at, 0:pad] = values[nlon - pad :]
            padded[at, pad + nlon :] = values[:pad]

        for c in range(cycles):
            place(c + 1, grid_v[c].astype(F32))

        @pl.when(rank > 0)
        def _():
            await_recv(halo.at[0], BEFORE)
            place(0, halo[0].astype(F32))

        @pl.when(rank == 0)
        def _():
            padded[0] = jnp.zeros(padded.shape[1:], F32)

        @pl.when(rank < R - 1)
        def _():
            await_recv(halo.at[1], AFTER)
            place(cycles + 1, halo[1].astype(F32))

        @pl.when(rank == R - 1)
        def _():
            padded[cycles + 1] = jnp.zeros(padded.shape[1:], F32)

        taps = conv_in.shape[0]
        block = 5 * TILE if nlon % (5 * TILE) == 0 else TILE

        def sine(cycle):
            angle = jnp.full((1, width), cycle, jnp.int32).astype(F32)
            return jnp.sin(math.pi * (angle + 0.5) / (R * cycles))

        for c in range(cycles):
            own = rank * cycles + c
            here = sine(own)
            weights = [
                conv_in[tap : tap + 1, :] * (sine(own + lat_off[tap]) / here)
                for tap in range(taps)
            ]

            @pl.loop(0, nlon // block)
            def _(b):
                base = pl.multiple_of(b * block, TILE)
                total = padded[c + 1, pl.ds(pad + base, block), :]
                for tap in range(taps):
                    source = padded[
                        c + 1 + lat_off[tap], pl.ds(pad + base + lon_off[tap], block), :
                    ]
                    total = total + weights[tap] * source
                local_send[c, pl.ds(base, block), :] = total.astype(BF16)

        @pl.loop(1, Y)
        def _(i):
            other = lax.rem(y + i, Y)
            first = pl.multiple_of(other * step, TILE)
            send(
                local_send.at[:, pl.ds(first, size)],
                local_recv.at[y],
                LOCAL,
                {"chan": other},
            )

        mine = pl.multiple_of(y * step, TILE)
        local_recv[y] = local_send[:, pl.ds(mine, size)]

    to_wavenumbers(0)
    local_field()
    for c in range(1, cycles):
        to_wavenumbers(c)
        legendre(c - 1)
    legendre(cycles - 1)

    gain = jnp.transpose(jnp.broadcast_to(gain_in[...], (width, L)))
    gain = jnp.concatenate([gain, gain], axis=1)
    for j in range(modes):
        weight = jnp.where(rank * modes + j == 0, 1.0, 2.0).astype(F32)
        scaled[j] = (acc[j] * gain * weight).astype(BF16)
    for c in range(cycles):
        for j in range(modes):
            back = jnp.dot(
                leg_t[j, c * Q * Z : (c + 1) * Q * Z, :], scaled[j], preferred_element_type=F32
            ).astype(BF16)
            for part in range(2):
                piece = back[:, part * width : (part + 1) * width]
                x2_send[c, :, 2 * j + part] = piece.reshape(Q, Z, width)
        send_q(x2_send, x2_recv, c, X2)

    for c in range(cycles):
        await_recv(x2_recv.at[c, pl.ds(0, Q - 1)], X2 + c)
        parts = [
            x2_recv[c, a, 2 * j + part].astype(F32)
            for part in range(2)
            for a in range(Q)
            for j in range(modes)
        ]
        z2_send[c] = jnp.swapaxes(jnp.stack(parts), 0, 1).astype(BF16)
        send_z(z2_send, z2_recv, c, Z2)

    copies[4].wait()
    copies[5].wait()
    copies[6].wait()
    await_recv(mix_all.at[pl.ds(0, Y - 1)], MIX)
    await_recv(local_recv.at[pl.ds(0, Y - 1)], LOCAL)

    def to_points(c):
        await_recv(z2_recv.at[c, pl.ds(0, Z - 1)], Z2 + c)
        value = z2_recv[c]
        wide = value.astype(F32)
        turned = jnp.concatenate([-wide[:, half:], wide[:, :half]], axis=1).astype(BF16)
        both = jnp.concatenate(
            [value.reshape(Z * rows, width), turned.reshape(Z * rows, width)], axis=1
        )
        fields = jnp.dot(inverse[...], both, preferred_element_type=F32).astype(BF16)
        field_send[c, 0] = fields[:, :width]
        field_send[c, 1] = fields[:, width:]

        @pl.loop(1, Y)
        def _(i):
            other = lax.rem(y + i, Y)
            first = pl.multiple_of(other * step, TILE)
            send(
                field_send.at[c, :, pl.ds(first, size)],
                field_recv.at[c, y],
                FIELD + c,
                {"chan": other},
            )

        mine = pl.multiple_of(y * step, TILE)
        field_recv[c, y] = field_send[c, :, pl.ds(mine, size)]

    def perceptron(c):
        await_recv(field_recv.at[c, pl.ds(0, Y - 1)], FIELD + c)
        points = jnp.concatenate(
            [field_recv[c, a, part] for part in range(2) for a in range(Y)], axis=1
        )
        pieces = []
        for a in range(Y):
            weights = jnp.concatenate([mix_all[a, 0], mix_all[a, 1]], axis=0)
            pieces.append(jnp.dot(points, weights, preferred_element_type=F32))
        spectral = jnp.concatenate(pieces, axis=1)
        near = jnp.concatenate([local_recv[a, c] for a in range(Y)], axis=1)
        row = (spectral + near.astype(F32)).astype(BF16).astype(F32)
        center = jnp.mean(row, axis=-1, keepdims=True)
        off = row - center
        spread = jnp.mean(off * off, axis=-1, keepdims=True)
        normed = (off / jnp.sqrt(spread + 1e-05) * norm_in[...]).astype(BF16)
        hidden = jax.nn.gelu(
            jnp.dot(normed, up_w[...], preferred_element_type=F32), approximate=True
        ).astype(BF16)
        result = (jnp.dot(hidden, down_w[...], preferred_element_type=F32) + row).astype(BF16)
        for a in range(Y):
            out_send[c, a] = result[:, a * width : (a + 1) * width]
        mine = pl.multiple_of(y * step, TILE)

        @pl.loop(1, Y)
        def _(i):
            other = lax.rem(y + i, Y)
            send(
                out_send.at[c, other, pl.ds(0, step)],
                out_recv.at[c, pl.ds(mine, step)],
                OUT + c,
                {"chan": other},
            )

            @pl.when(y == Y - 1)
            def _():
                send(
                    out_send.at[c, other, pl.ds(step, size - step)],
                    out_recv.at[c, pl.ds(Y * step, size - step)],
                    EXTRA + c,
                    {"chan": other},
                )

        out_recv[c, pl.ds(mine, step), :] = out_send[c, y, 0:step]

        @pl.when(y == Y - 1)
        def _():
            out_recv[c, Y * step :, :] = out_send[c, y, step:]

    def finish(c):
        await_recv(out_recv.at[c, pl.ds(0, (Y - 1) * step)], OUT + c)

        @pl.when(y < Y - 1)
        def _():
            await_recv(out_recv.at[c, pl.ds(0, size - step)], EXTRA + c)

        pltpu.make_async_copy(out_recv.at[c], out.at[c], load_sem.at[len(loads) + c]).start()

    to_points(0)
    for c in range(1, cycles):
        to_points(c)
        perceptron(c - 1)
        if c > 1:
            finish(c - 2)
    perceptron(cycles - 1)
    finish(cycles - 2)
    finish(cycles - 1)

    for c in range(cycles):
        await_send(z1_send.at[c, pl.ds(0, Z - 1)], Z1 + c)
        await_send(z2_send.at[c, pl.ds(0, Z - 1)], Z2 + c)
        await_send(x1_send.at[c, pl.ds(0, Q - 1)], X1 + c)
        await_send(x2_send.at[c, pl.ds(0, Q - 1)], X2 + c)
        await_send(field_recv.at[c, pl.ds(0, Y - 1)], FIELD + c)
        await_send(out_recv.at[c, pl.ds(0, (Y - 1) * step)], OUT + c)

        @pl.when(y == Y - 1)
        def _():
            await_send(out_recv.at[c, pl.ds(0, (Y - 1) * (size - step))], EXTRA + c)

    await_send(local_recv.at[pl.ds(0, Y - 1)], LOCAL)
    await_send(mix_all.at[pl.ds(0, Y - 1)], MIX)

    @pl.when(rank < R - 1)
    def _():
        await_send(halo.at[0], BEFORE)

    @pl.when(rank > 0)
    def _():
        await_send(halo.at[1], AFTER)

    for c in range(cycles):
        pltpu.make_async_copy(out_recv.at[c], out.at[c], load_sem.at[len(loads) + c]).wait()


def on_device(
    sizes,
    grid,
    basis,
    mix_weight,
    spectral_gain,
    conv_weight,
    lat_offsets,
    lon_offsets,
    ln_gain,
    up_weight,
    down_weight,
):
    X, Z, K, Y = sizes
    cycles, nlon, width = grid.shape
    modes, L, nlat = basis.shape
    C = width * Y
    Q = X * K
    step = nlon // (Y * TILE) * TILE
    size = nlon - (Y - 1) * step
    rows = 2 * Q * modes
    table = transform_tables(X, Z, K, modes, nlon)
    inverse = np.ascontiguousarray(table.T)
    order = cycle_order(X, Z, K, cycles)
    perm = np.zeros((nlat, nlat), ml_dtypes.bfloat16)
    perm[np.arange(nlat), order] = 1
    theta = (math.pi * (np.arange(nlat, dtype=np.float32) + np.float32(0.5)) / nlat).astype(
        np.float32
    )
    quad = (np.float32(math.pi / nlat) * np.sin(theta)).astype(np.float32)[None, :]
    dims = (X, Z, K, Y, cycles, modes, L, nlon, width, step, size)
    any_space = pl.BlockSpec(memory_space=pl.ANY)
    vmem = pl.BlockSpec(memory_space=pltpu.VMEM)
    smem = pl.BlockSpec(memory_space=pltpu.SMEM)
    pad = 8
    n_sem = 7 * cycles + 4
    scratch = [
        pltpu.VMEM((cycles, nlon, width), BF16),
        pltpu.VMEM(table.shape, BF16),
        pltpu.VMEM(inverse.shape, BF16),
        pltpu.VMEM(perm.shape, BF16),
        pltpu.VMEM(basis.shape, F32),
        pltpu.VMEM((Y, 2, C, width), BF16),
        pltpu.VMEM(up_weight.shape, BF16),
        pltpu.VMEM(down_weight.shape, BF16),
        pltpu.VMEM((modes, L, nlat), BF16),
        pltpu.VMEM((modes, nlat, L), BF16),
        pltpu.VMEM((cycles, Z, rows, width), BF16),
        pltpu.VMEM((cycles, Z, rows, width), BF16),
        pltpu.VMEM((cycles, Q, 2 * modes, Z, width), BF16),
        pltpu.VMEM((cycles, Q, 2 * modes, Z, width), BF16),
        pltpu.VMEM((modes, L, 2 * width), F32),
        pltpu.VMEM((modes, L, 2 * width), BF16),
        pltpu.VMEM((cycles, Q, 2 * modes, Z, width), BF16),
        pltpu.VMEM((cycles, Q, 2 * modes, Z, width), BF16),
        pltpu.VMEM((cycles, Z, rows, width), BF16),
        pltpu.VMEM((cycles, Z, rows, width), BF16),
        pltpu.VMEM((2, nlon, width), BF16),
        pltpu.VMEM((cycles + 2, nlon + 2 * pad, width), F32),
        pltpu.VMEM((cycles, nlon, width), BF16),
        pltpu.VMEM((Y, cycles, size, width), BF16),
        pltpu.VMEM((cycles, 2, nlon, width), BF16),
        pltpu.VMEM((cycles, Y, 2, size, width), BF16),
        pltpu.VMEM((cycles, Y, size, width), BF16),
        pltpu.VMEM((cycles, nlon, width), BF16),
        pltpu.SemaphoreType.DMA((8 + cycles,)),
        pltpu.SemaphoreType.DMA((n_sem,)),
        pltpu.SemaphoreType.DMA((n_sem,)),
    ]
    return pl.pallas_call(
        functools.partial(block_kernel, dims),
        out_shape=jax.ShapeDtypeStruct(grid.shape, BF16),
        in_specs=[any_space] * 6
        + [vmem, vmem, vmem, smem, smem, vmem]
        + [any_space] * 2,
        out_specs=any_space,
        scratch_shapes=scratch,
        compiler_params=pltpu.CompilerParams(
            collective_id=0, has_side_effects=True, vmem_limit_bytes=56 * 1024 * 1024
        ),
        name="block",
    )(
        grid,
        jnp.asarray(table),
        jnp.asarray(inverse),
        jnp.asarray(perm),
        basis,
        mix_weight,
        spectral_gain.reshape(1, L),
        jnp.asarray(quad),
        conv_weight,
        lat_offsets,
        lon_offsets,
        ln_gain.reshape(1, C),
        up_weight,
        down_weight,
    )


def build(finer):
    sizes = tuple(finer.shape[a] for a in (*LAT, "chan"))
    return jax.shard_map(
        functools.partial(on_device, sizes),
        mesh=finer,
        in_specs=(
            P(LAT, None, "chan"),
            P(LAT, None, None),
            P(None, None, "chan"),
            P(),
            P(None, "chan"),
            P(),
            P(),
            P(),
            P(),
            P(),
        ),
        out_specs=P(LAT, None, "chan"),
        check_vma=False,
    )


def solution(mesh):
    return build(
        Mesh(mesh.devices.reshape(4, 16, 2, mesh.shape["chan"]), (*LAT, "chan"))
    )
```

```python
import functools
import math

import jax
import jax.numpy as jnp
import ml_dtypes
import numpy as np
from jax import lax
from jax.experimental import pallas as pl
from jax.experimental.pallas import tpu as pltpu
from jax.sharding import Mesh
from jax.sharding import PartitionSpec as P

LAT = ("lat_0", "lat_1", "lat_2")
MESH_ID = pl.DeviceIdType.MESH
TILE = 16
F32 = jnp.float32
BF16 = jnp.bfloat16


def transform_tables(X, Z, K, modes, nlon):
    j, z, ri, x, k = np.meshgrid(
        np.arange(modes), np.arange(Z), np.arange(2), np.arange(X), np.arange(K), indexing="ij"
    )
    m = (((x * Z + z) * K + k) * modes + j).reshape(modes, -1).astype(np.int64)
    part = ri.reshape(modes, -1)
    points = np.arange(nlon, dtype=np.int64)
    phase = (m[:, :, None] * points) % nlon
    angle = np.float32(2.0 * math.pi) * phase.astype(np.float32) / np.float32(nlon)
    table = np.where(part[:, :, None] == 0, np.cos(angle), -np.sin(angle)).astype(np.float32)
    return table.astype(ml_dtypes.bfloat16)


def cycle_order(X, Z, K, cycles):
    x, k, z, c = np.meshgrid(
        np.arange(X), np.arange(K), np.arange(Z), np.arange(cycles), indexing="ij"
    )
    return (((x * Z + z) * K + k) * cycles + c).reshape(-1)


def block_kernel(
    dims,
    grid_in,
    table_in,
    inverse_in,
    perm_in,
    basis_in,
    mix_in,
    gain_in,
    quad_in,
    conv_in,
    lat_off,
    lon_off,
    norm_in,
    up_in,
    down_in,
    out,
    grid_v,
    table,
    inverse,
    perm,
    basis,
    mix_v,
    mix_w,
    up_w,
    down_w,
    leg,
    leg_t,
    z1_send,
    z1_recv,
    x1_send,
    x1_recv,
    coeff,
    x2_send,
    x2_recv,
    z2_send,
    z2_recv,
    halo,
    padded,
    base,
    sum_send,
    sum_recv,
    out_send,
    out_recv,
    load_sem,
    send_sem,
    recv_sem,
):
    X, Z, K, Y, cycles, modes, L, nlon, width, step, size = dims
    Q = X * K
    R = Q * Z
    band = Z * cycles
    x = lax.axis_index("lat_0")
    z = lax.axis_index("lat_1")
    k = lax.axis_index("lat_2")
    y = lax.axis_index("chan")
    q = x * K + k
    rank = (x * Z + z) * K + k
    last = modes - 1
    pad = (padded.shape[1] - nlon) // 2

    loads = [(table_in.at[0], table.at[0]), (grid_in, grid_v)]
    loads += [(table_in.at[j], table.at[j]) for j in range(1, modes)]
    BASIS = len(loads)
    loads += [(basis_in, basis), (perm_in, perm), (mix_in, mix_v)]
    REST = len(loads)
    loads += [(inverse_in, inverse), (up_in, up_w), (down_in, down_w)]
    copies = [
        pltpu.make_async_copy(src, dst, load_sem.at[i]) for i, (src, dst) in enumerate(loads)
    ]
    def q_device(other):
        return {"lat_0": other // K, "lat_2": lax.rem(other, K)}

    def rank_device(r):
        return {"lat_0": r // (Z * K), "lat_1": lax.rem(r // K, Z), "lat_2": lax.rem(r, K)}

    barrier = pltpu.get_barrier_semaphore()

    def greet(device):
        pl.semaphore_signal(barrier, inc=1, device_id=device, device_id_type=MESH_ID)

    def ring_place(i):
        far = Z - 1 - i
        offset = jnp.where(lax.rem(far, 2) == 1, (far + 1) // 2, Z - far // 2)
        return lax.rem(z + offset, Z)

    @pl.loop(0, Z - 1)
    def _(i):
        greet({"lat_1": ring_place(i)})

    copies[0].start()
    copies[1].start()

    @pl.loop(1, Q)
    def _(i):
        greet(q_device(lax.rem(q + i, Q)))

    @pl.loop(1, Y)
    def _(i):
        greet({"chan": lax.rem(y + i, Y)})

    @pl.when(rank > 0)
    def _():
        greet(rank_device(rank - 1))

    @pl.when(rank < R - 1)
    def _():
        greet(rank_device(rank + 1))

    def send(src, dst, at, device):
        pltpu.make_async_remote_copy(
            src_ref=src,
            dst_ref=dst,
            send_sem=send_sem.at[at],
            recv_sem=recv_sem.at[at],
            device_id=device,
            device_id_type=MESH_ID,
        ).start()

    def await_recv(ref, at):
        pltpu.make_async_copy(ref, ref, recv_sem.at[at]).wait()

    def await_send(ref, at):
        pltpu.make_async_copy(ref, ref, send_sem.at[at]).wait()

    Z1, X1, X2, Z2, GATHER = (n * modes for n in range(5))
    LAST = 5 * modes
    SUM = LAST + cycles
    OUT = SUM + cycles
    EXTRA = OUT + cycles
    BEFORE = EXTRA + cycles
    AFTER = BEFORE + 1

    def forward(j):
        points = jnp.concatenate([grid_v[c] for c in range(cycles)], axis=1)
        spec = jnp.dot(table[j], points, preferred_element_type=F32) * (1.0 / nlon)
        spec = spec.astype(BF16)
        for c in range(cycles):
            z1_send[j, :, c] = spec[:, c * width : (c + 1) * width].reshape(Z, 2 * Q, width)

    def send_z(buf, land, j, at):
        @pl.loop(0, Z - 1)
        def _(i):
            other = ring_place(i)
            send(buf.at[j, other], land.at[j, z], at + j, {"lat_1": other})

        land[j, z] = buf[j, z]

    def send_q(buf, land, j, at):
        @pl.loop(1, Q)
        def _(i):
            other = lax.rem(q + i, Q)
            send(buf.at[j, other], land.at[j, q], at + j, q_device(other))

        land[j, q] = buf[j, q]

    copies[0].wait()
    copies[1].wait()
    for copy in copies[2:]:
        copy.start()
    forward(0)
    greeted = (Z - 1) + (Q - 1) + (Y - 1)
    greeted = greeted + jnp.where(rank > 0, 1, 0) + jnp.where(rank < R - 1, 1, 0)
    pl.semaphore_wait(barrier, greeted)
    send_z(z1_send, z1_recv, 0, Z1)

    for j in range(1, modes):
        copies[1 + j].wait()
        forward(j)
        send_z(z1_send, z1_recv, j, Z1)

    @pl.when(rank < R - 1)
    def _():
        send(grid_v.at[cycles - 1], halo.at[0], BEFORE, rank_device(rank + 1))

    @pl.when(rank > 0)
    def _():
        send(grid_v.at[0], halo.at[1], AFTER, rank_device(rank - 1))

    copies[BASIS].wait()
    copies[BASIS + 1].wait()
    for j in range(modes):
        weighted = (basis[j] * quad_in[...]).astype(BF16)
        leg[j] = lax.dot_general(
            weighted, perm[...], (((1,), (1,)), ((), ())), preferred_element_type=F32
        ).astype(BF16)
        leg_t[j] = lax.dot_general(
            perm[...], basis[j].astype(BF16), (((1,), (1,)), ((), ())), preferred_element_type=F32
        ).astype(BF16)
    copies[BASIS + 2].wait()
    for a in range(Y):
        real = mix_v[0, a * width : (a + 1) * width, :]
        imag = mix_v[1, a * width : (a + 1) * width, :]
        at = 2 * a * width
        mix_w[at : at + width, :width] = real
        mix_w[at : at + width, width:] = imag
        mix_w[at + width : at + 2 * width, :width] = -imag
        mix_w[at + width : at + 2 * width, width:] = real
    gain = jnp.transpose(jnp.broadcast_to(gain_in[...].reshape(1, L), (width, L)))

    def to_owners(j):
        await_recv(z1_recv.at[j, pl.ds(0, Z - 1)], Z1 + j)
        value = z1_recv[j].reshape(band, 2 * Q, width)
        turned = jnp.swapaxes(value.astype(F32), 0, 1).astype(BF16)
        for part in range(2):
            x1_send[j, :, part] = turned[part * Q : (part + 1) * Q]
        send_q(x1_send, x1_recv, j, X1)

    def legendre(j):
        await_recv(x1_recv.at[j, pl.ds(0, Q - 1)], X1 + j)
        parts = [x1_recv[j, :, part].reshape(Q * band, width) for part in range(2)]
        values = jnp.concatenate(parts, axis=1)
        coeff[j, y] = jnp.dot(leg[j], values, preferred_element_type=F32).astype(BF16)

        @pl.loop(1, Y)
        def _(i):
            send(coeff.at[j, y], coeff.at[j, y], GATHER + j, {"chan": lax.rem(y + i, Y)})

    def mix(j):
        await_recv(coeff.at[j, pl.ds(0, Y - 1)], GATHER + j)
        values = jnp.concatenate([coeff[j, a] for a in range(Y)], axis=1)
        mixed = jnp.dot(values, mix_w[...], preferred_element_type=F32)
        weight = jnp.where(rank * modes + j == 0, 1.0, 2.0).astype(F32)
        scale = gain * weight
        mixed = (mixed * jnp.concatenate([scale, scale], axis=1)).astype(BF16)
        back = jnp.dot(leg_t[j], mixed, preferred_element_type=F32).astype(BF16)
        for part in range(2):
            piece = back[:, part * width : (part + 1) * width]
            x2_send[j, :, part] = piece.reshape(Q, band, width)
        send_q(x2_send, x2_recv, j, X2)

    def to_cycles(j):
        await_recv(x2_recv.at[j, pl.ds(0, Q - 1)], X2 + j)
        parts = [x2_recv[j, a, part].astype(F32) for part in range(2) for a in range(Q)]
        turned = jnp.swapaxes(jnp.stack(parts), 0, 1).astype(BF16)
        z2_send[j] = turned.reshape(Z, cycles, 2 * Q, width)
        if j < last:
            send_z(z2_send, z2_recv, j, Z2)
        else:
            for c in range(cycles):

                @pl.loop(0, Z - 1)
                def _(i):
                    other = ring_place(i)
                    send(
                        z2_send.at[j, other, c],
                        z2_recv.at[j, z, c],
                        LAST + c,
                        {"lat_1": other},
                    )

            z2_recv[j, z] = z2_send[j, z]

    def place(at, values):
        padded[at, pad : pad + nlon] = values
        padded[at, 0:pad] = values[nlon - pad :]
        padded[at, pad + nlon :] = values[:pad]

    def pad_field():
        for c in range(cycles):
            place(c + 1, grid_v[c].astype(F32))

        @pl.when(rank > 0)
        def _():
            await_recv(halo.at[0], BEFORE)
            place(0, halo[0].astype(F32))

        @pl.when(rank == 0)
        def _():
            padded[0] = jnp.zeros(padded.shape[1:], F32)

        @pl.when(rank < R - 1)
        def _():
            await_recv(halo.at[1], AFTER)
            place(cycles + 1, halo[1].astype(F32))

        @pl.when(rank == R - 1)
        def _():
            padded[cycles + 1] = jnp.zeros(padded.shape[1:], F32)

    def sine(cycle):
        angle = jnp.full((1, width), cycle, jnp.int32).astype(F32)
        return jnp.sin(math.pi * (angle + 0.5) / (R * cycles))

    def local_field(c):
        taps = conv_in.shape[0]
        block = 5 * TILE if nlon % (5 * TILE) == 0 else TILE
        own = rank * cycles + c
        here = sine(own)
        weights = [
            conv_in[tap : tap + 1, :] * (sine(own + lat_off[tap]) / here) for tap in range(taps)
        ]

        @pl.loop(0, nlon // block)
        def _(b):
            first = pl.multiple_of(b * block, TILE)
            total = padded[c + 1, pl.ds(pad + first, block), :]
            for tap in range(taps):
                source = padded[c + 1 + lat_off[tap], pl.ds(pad + first + lon_off[tap], block), :]
                total = total + weights[tap] * source
            base[c, pl.ds(first, block), :] = total

    to_owners(0)
    legendre(0)
    for j in range(1, modes):
        to_owners(j)
        if j > 1:
            mix(j - 2)
        legendre(j)
        if j > 1:
            to_cycles(j - 2)
    for j in range(last - 1, modes):
        mix(j)
        to_cycles(j)
    pad_field()
    for c in range(cycles):
        local_field(c)
    for i in range(3):
        copies[REST + i].wait()

    def synthesize(j):
        await_recv(z2_recv.at[j, pl.ds(0, Z - 1)], Z2 + j)
        values = jnp.concatenate(
            [z2_recv[j, :, c].reshape(2 * R, width) for c in range(cycles)], axis=1
        )
        found = jnp.dot(inverse[j], values, preferred_element_type=F32)
        for c in range(cycles):
            base[c] += found[:, c * width : (c + 1) * width]

    mine = pl.multiple_of(y * step, TILE)

    def to_points(c):
        await_recv(z2_recv.at[last, pl.ds(0, Z - 1), c], LAST + c)
        value = z2_recv[last, :, c].reshape(2 * R, width)
        found = jnp.dot(inverse[last], value, preferred_element_type=F32)
        sum_send[c] = (base[c] + found).astype(BF16)

        @pl.loop(1, Y)
        def _(i):
            other = lax.rem(y + i, Y)
            first = pl.multiple_of(other * step, TILE)
            send(
                sum_send.at[c, pl.ds(first, size)], sum_recv.at[c, y], SUM + c, {"chan": other}
            )

        sum_recv[c, y] = sum_send[c, pl.ds(mine, size)]

    def perceptron(c):
        await_recv(sum_recv.at[c, pl.ds(0, Y - 1)], SUM + c)
        row = jnp.concatenate([sum_recv[c, a] for a in range(Y)], axis=1).astype(F32)
        center = jnp.mean(row, axis=-1, keepdims=True)
        off = row - center
        spread = jnp.mean(off * off, axis=-1, keepdims=True)
        normed = (off / jnp.sqrt(spread + 1e-05) * norm_in[...]).astype(BF16)
        hidden = jax.nn.gelu(
            jnp.dot(normed, up_w[...], preferred_element_type=F32), approximate=True
        ).astype(BF16)
        result = (jnp.dot(hidden, down_w[...], preferred_element_type=F32) + row).astype(BF16)
        for a in range(Y):
            out_send[c, a] = result[:, a * width : (a + 1) * width]

        @pl.loop(1, Y)
        def _(i):
            other = lax.rem(y + i, Y)
            send(
                out_send.at[c, other, pl.ds(0, step)],
                out_recv.at[c, pl.ds(mine, step)],
                OUT + c,
                {"chan": other},
            )

            @pl.when(y == Y - 1)
            def _():
                send(
                    out_send.at[c, other, pl.ds(step, size - step)],
                    out_recv.at[c, pl.ds(Y * step, size - step)],
                    EXTRA + c,
                    {"chan": other},
                )

        out_recv[c, pl.ds(mine, step), :] = out_send[c, y, 0:step]

        @pl.when(y == Y - 1)
        def _():
            out_recv[c, Y * step :, :] = out_send[c, y, step:]

    def finish(c):
        await_recv(out_recv.at[c, pl.ds(0, (Y - 1) * step)], OUT + c)

        @pl.when(y < Y - 1)
        def _():
            await_recv(out_recv.at[c, pl.ds(0, size - step)], EXTRA + c)

        pltpu.make_async_copy(out_recv.at[c], out.at[c], load_sem.at[len(loads) + c]).start()

    for j in range(last):
        synthesize(j)
    to_points(0)
    for c in range(1, cycles):
        to_points(c)
        perceptron(c - 1)
    perceptron(cycles - 1)
    for c in range(cycles):
        finish(c)

    for j in range(modes):
        await_send(z1_send.at[j, pl.ds(0, Z - 1)], Z1 + j)
        await_send(x1_send.at[j, pl.ds(0, Q - 1)], X1 + j)
        await_send(x2_send.at[j, pl.ds(0, Q - 1)], X2 + j)
        if j < last:
            await_send(z2_send.at[j, pl.ds(0, Z - 1)], Z2 + j)
        await_send(coeff.at[j, pl.ds(0, Y - 1)], GATHER + j)
    for c in range(cycles):
        await_send(z2_send.at[last, pl.ds(0, Z - 1), c], LAST + c)
        await_send(sum_recv.at[c, pl.ds(0, Y - 1)], SUM + c)
        await_send(out_recv.at[c, pl.ds(0, (Y - 1) * step)], OUT + c)

        @pl.when(y == Y - 1)
        def _():
            await_send(out_recv.at[c, pl.ds(0, (Y - 1) * (size - step))], EXTRA + c)

    @pl.when(rank < R - 1)
    def _():
        await_send(halo.at[0], BEFORE)

    @pl.when(rank > 0)
    def _():
        await_send(halo.at[1], AFTER)

    for c in range(cycles):
        pltpu.make_async_copy(out_recv.at[c], out.at[c], load_sem.at[len(loads) + c]).wait()


def on_device(
    sizes,
    grid,
    basis,
    mix_weight,
    spectral_gain,
    conv_weight,
    lat_offsets,
    lon_offsets,
    ln_gain,
    up_weight,
    down_weight,
):
    X, Z, K, Y = sizes
    cycles, nlon, width = grid.shape
    modes, L, nlat = basis.shape
    C = width * Y
    Q = X * K
    step = nlon // (Y * TILE) * TILE
    size = nlon - (Y - 1) * step
    table = transform_tables(X, Z, K, modes, nlon)
    inverse = np.ascontiguousarray(table.transpose(0, 2, 1))
    perm = np.zeros((nlat, nlat), ml_dtypes.bfloat16)
    perm[np.arange(nlat), cycle_order(X, Z, K, cycles)] = 1
    theta = (math.pi * (np.arange(nlat, dtype=np.float32) + np.float32(0.5)) / nlat).astype(
        np.float32
    )
    quad = (np.float32(math.pi / nlat) * np.sin(theta)).astype(np.float32)[None, :]
    dims = (X, Z, K, Y, cycles, modes, L, nlon, width, step, size)
    any_space = pl.BlockSpec(memory_space=pl.ANY)
    vmem = pl.BlockSpec(memory_space=pltpu.VMEM)
    smem = pl.BlockSpec(memory_space=pltpu.SMEM)
    pad = 8
    n_sem = 5 * modes + 4 * cycles + 2
    around_z = (modes, Z, cycles, 2 * Q, width)
    around_q = (modes, Q, 2, Z * cycles, width)
    scratch = [
        pltpu.VMEM((cycles, nlon, width), BF16),
        pltpu.VMEM(table.shape, BF16),
        pltpu.VMEM(inverse.shape, BF16),
        pltpu.VMEM(perm.shape, BF16),
        pltpu.VMEM(basis.shape, F32),
        pltpu.VMEM(mix_weight.shape, BF16),
        pltpu.VMEM((2 * C, 2 * width), BF16),
        pltpu.VMEM(up_weight.shape, BF16),
        pltpu.VMEM(down_weight.shape, BF16),
        pltpu.VMEM((modes, L, nlat), BF16),
        pltpu.VMEM((modes, nlat, L), BF16),
        pltpu.VMEM(around_z, BF16),
        pltpu.VMEM(around_z, BF16),
        pltpu.VMEM(around_q, BF16),
        pltpu.VMEM(around_q, BF16),
        pltpu.VMEM((modes, Y, L, 2 * width), BF16),
        pltpu.VMEM(around_q, BF16),
        pltpu.VMEM(around_q, BF16),
        pltpu.VMEM(around_z, BF16),
        pltpu.VMEM(around_z, BF16),
        pltpu.VMEM((2, nlon, width), BF16),
        pltpu.VMEM((cycles + 2, nlon + 2 * pad, width), F32),
        pltpu.VMEM((cycles, nlon, width), F32),
        pltpu.VMEM((cycles, nlon, width), BF16),
        pltpu.VMEM((cycles, Y, size, width), BF16),
        pltpu.VMEM((cycles, Y, size, width), BF16),
        pltpu.VMEM((cycles, nlon, width), BF16),
        pltpu.SemaphoreType.DMA((7 + modes + cycles,)),
        pltpu.SemaphoreType.DMA((n_sem,)),
        pltpu.SemaphoreType.DMA((n_sem,)),
    ]
    return pl.pallas_call(
        functools.partial(block_kernel, dims),
        out_shape=jax.ShapeDtypeStruct(grid.shape, BF16),
        in_specs=[any_space] * 6
        + [vmem, vmem, vmem, smem, smem, vmem]
        + [any_space] * 2,
        out_specs=any_space,
        scratch_shapes=scratch,
        compiler_params=pltpu.CompilerParams(
            collective_id=0, has_side_effects=True, vmem_limit_bytes=56 * 1024 * 1024
        ),
        name="block",
    )(
        grid,
        jnp.asarray(table),
        jnp.asarray(inverse),
        jnp.asarray(perm),
        basis,
        mix_weight,
        spectral_gain,
        jnp.asarray(quad),
        conv_weight,
        lat_offsets,
        lon_offsets,
        ln_gain.reshape(1, C),
        up_weight,
        down_weight,
    )


def build(finer):
    sizes = tuple(finer.shape[a] for a in (*LAT, "chan"))
    return jax.shard_map(
        functools.partial(on_device, sizes),
        mesh=finer,
        in_specs=(
            P(LAT, None, "chan"),
            P(LAT, None, None),
            P(None, None, "chan"),
            P(),
            P(None, "chan"),
            P(),
            P(),
            P(),
            P(),
            P(),
        ),
        out_specs=P(LAT, None, "chan"),
        check_vma=False,
    )


def solution(mesh):
    return build(
        Mesh(mesh.devices.reshape(4, 16, 2, mesh.shape["chan"]), (*LAT, "chan"))
    )
```

```python
import functools
import math

import jax
import jax.numpy as jnp
import ml_dtypes
import numpy as np
from jax import lax
from jax.experimental import pallas as pl
from jax.experimental.pallas import tpu as pltpu
from jax.sharding import Mesh
from jax.sharding import PartitionSpec as P

LAT = ("lat_0", "lat_1", "lat_2")
MESH_ID = pl.DeviceIdType.MESH
TILE = 16
F32 = jnp.float32
BF16 = jnp.bfloat16


def transform_tables(X, Z, K, modes, nlon):
    j, z, ri, x, k = np.meshgrid(
        np.arange(modes), np.arange(Z), np.arange(2), np.arange(X), np.arange(K), indexing="ij"
    )
    m = (((x * Z + z) * K + k) * modes + j).reshape(modes, -1).astype(np.int64)
    part = ri.reshape(modes, -1)
    points = np.arange(nlon, dtype=np.int64)
    phase = (m[:, :, None] * points) % nlon
    angle = np.float32(2.0 * math.pi) * phase.astype(np.float32) / np.float32(nlon)
    table = np.where(part[:, :, None] == 0, np.cos(angle), -np.sin(angle)).astype(np.float32)
    return table.astype(ml_dtypes.bfloat16)


def cycle_order(X, Z, K, cycles):
    c, x, k, z = np.meshgrid(
        np.arange(cycles), np.arange(X), np.arange(K), np.arange(Z), indexing="ij"
    )
    return (((x * Z + z) * K + k) * cycles + c).reshape(-1)


def block_kernel(
    dims,
    grid_in,
    table_in,
    inverse_in,
    perm_in,
    basis_in,
    mix_in,
    gain_in,
    quad_in,
    conv_in,
    lat_off,
    lon_off,
    norm_in,
    up_in,
    down_in,
    out,
    grid_v,
    table,
    inverse,
    perm,
    basis,
    mix_all,
    mix_w,
    up_w,
    down_w,
    leg,
    leg_t,
    z1_send,
    z1_recv,
    x1_send,
    x1_recv,
    gathered,
    x2_send,
    x2_recv,
    z2_send,
    z2_recv,
    halo,
    padded,
    base,
    local_send,
    local_recv,
    field_send,
    field_recv,
    sum_send,
    sum_recv,
    out_send,
    load_sem,
    send_sem,
    recv_sem,
):
    X, Z, K, Y, cycles, modes, L, nlon, width, step, size = dims
    Q = X * K
    R = Q * Z
    x = lax.axis_index("lat_0")
    z = lax.axis_index("lat_1")
    k = lax.axis_index("lat_2")
    y = lax.axis_index("chan")
    q = x * K + k
    rank = (x * Z + z) * K + k
    last = modes - 1
    early = pl.ds(0, last)
    rest = pl.ds(1, cycles - 1)
    plane = Q * Z
    pad = (padded.shape[1] - nlon) // 2

    loads = [(table_in.at[0], table.at[0]), (grid_in, grid_v)]
    loads += [(table_in.at[j], table.at[j]) for j in range(1, modes)]
    BASIS = len(loads)
    loads += [(basis_in, basis), (perm_in, perm), (mix_in, mix_all.at[y])]
    REST = len(loads)
    loads += [(inverse_in, inverse), (up_in, up_w), (down_in, down_w)]
    copies = [
        pltpu.make_async_copy(src, dst, load_sem.at[i]) for i, (src, dst) in enumerate(loads)
    ]
    def q_device(other):
        return {"lat_0": other // K, "lat_2": lax.rem(other, K)}

    def rank_device(r):
        return {"lat_0": r // (Z * K), "lat_1": lax.rem(r // K, Z), "lat_2": lax.rem(r, K)}

    barrier = pltpu.get_barrier_semaphore()

    def greet(device):
        pl.semaphore_signal(barrier, inc=1, device_id=device, device_id_type=MESH_ID)

    def ring_place(i):
        far = Z - 1 - i
        offset = jnp.where(lax.rem(far, 2) == 1, (far + 1) // 2, Z - far // 2)
        return lax.rem(z + offset, Z)

    @pl.loop(0, Z - 1)
    def _(i):
        greet({"lat_1": ring_place(i)})

    copies[0].start()
    copies[1].start()

    @pl.loop(1, Q)
    def _(i):
        greet(q_device(lax.rem(q + i, Q)))

    @pl.loop(1, Y)
    def _(i):
        greet({"chan": lax.rem(y + i, Y)})

    @pl.when(rank > 0)
    def _():
        greet(rank_device(rank - 1))

    @pl.when(rank < R - 1)
    def _():
        greet(rank_device(rank + 1))

    def send(src, dst, at, device):
        pltpu.make_async_remote_copy(
            src_ref=src,
            dst_ref=dst,
            send_sem=send_sem.at[at],
            recv_sem=recv_sem.at[at],
            device_id=device,
            device_id_type=MESH_ID,
        ).start()

    def await_recv(ref, at):
        pltpu.make_async_copy(ref, ref, recv_sem.at[at]).wait()

    def await_send(ref, at):
        pltpu.make_async_copy(ref, ref, send_sem.at[at]).wait()

    Z1, X1, X2, X2_REST, GATHER = (n * modes for n in range(5))
    EARLY = 5 * modes
    LAST = EARLY + cycles
    FIELD = LAST + cycles
    OUT = FIELD + cycles
    EXTRA = OUT + cycles
    LOCAL = EXTRA + cycles
    MIX = LOCAL + 1
    BEFORE = LOCAL + 2
    AFTER = LOCAL + 3

    def forward(j):
        points = jnp.concatenate([grid_v[c] for c in range(cycles)], axis=1)
        spec = jnp.dot(table[j], points, preferred_element_type=F32) * (1.0 / nlon)
        spec = spec.astype(BF16)
        for c in range(cycles):
            z1_send[j, :, c] = spec[:, c * width : (c + 1) * width].reshape(Z, 2 * Q, width)

    def send_z(buf, land, j, at):
        @pl.loop(0, Z - 1)
        def _(i):
            other = ring_place(i)
            send(buf.at[j, other], land.at[j, z], at + j, {"lat_1": other})

        land[j, z] = buf[j, z]

    def send_q(buf, land, j, at):
        @pl.loop(1, Q)
        def _(i):
            other = lax.rem(q + i, Q)
            send(buf.at[j, other], land.at[j, q], at + j, q_device(other))

        land[j, q] = buf[j, q]

    copies[0].wait()
    copies[1].wait()
    for copy in copies[2:]:
        copy.start()
    forward(0)
    greeted = (Z - 1) + (Q - 1) + (Y - 1)
    greeted = greeted + jnp.where(rank > 0, 1, 0) + jnp.where(rank < R - 1, 1, 0)
    pl.semaphore_wait(barrier, greeted)
    send_z(z1_send, z1_recv, 0, Z1)

    for j in range(1, modes):
        copies[1 + j].wait()
        forward(j)
        send_z(z1_send, z1_recv, j, Z1)

    @pl.when(rank < R - 1)
    def _():
        send(grid_v.at[cycles - 1], halo.at[0], BEFORE, rank_device(rank + 1))

    @pl.when(rank > 0)
    def _():
        send(grid_v.at[0], halo.at[1], AFTER, rank_device(rank - 1))

    copies[BASIS].wait()
    copies[BASIS + 1].wait()
    copies[BASIS + 2].wait()

    @pl.loop(1, Y)
    def _(i):
        send(mix_all.at[y], mix_all.at[y], MIX, {"chan": lax.rem(y + i, Y)})

    for j in range(modes):
        weighted = (basis[j] * quad_in[...]).astype(BF16)
        leg[j] = lax.dot_general(
            weighted, perm[...], (((1,), (1,)), ((), ())), preferred_element_type=F32
        ).astype(BF16)
        leg_t[j] = lax.dot_general(
            perm[...], basis[j].astype(BF16), (((1,), (1,)), ((), ())), preferred_element_type=F32
        ).astype(BF16)
    for a in range(Y):
        real = mix_all[y, 0, a * width : (a + 1) * width, :]
        imag = mix_all[y, 1, a * width : (a + 1) * width, :]
        at = 2 * a * width
        mix_w[at : at + width, :width] = real
        mix_w[at : at + width, width:] = imag
        mix_w[at + width : at + 2 * width, :width] = -imag
        mix_w[at + width : at + 2 * width, width:] = real
    gain = jnp.transpose(jnp.broadcast_to(gain_in[...].reshape(1, L), (width, L)))

    def to_owners(j):
        await_recv(z1_recv.at[j, pl.ds(0, Z - 1)], Z1 + j)
        for c in range(cycles):
            turned = jnp.swapaxes(z1_recv[j, :, c].astype(F32), 0, 1).astype(BF16)
            for part in range(2):
                x1_send[j, :, part, c] = turned[part * Q : (part + 1) * Q]
        send_q(x1_send, x1_recv, j, X1)

    def send_rows(j, cut, at):
        @pl.loop(1, Q)
        def _(i):
            other = lax.rem(q + i, Q)
            send(x2_send.at[j, other, cut], x2_recv.at[j, q, cut], at + j, q_device(other))

    def legendre(j):
        await_recv(x1_recv.at[j, pl.ds(0, Q - 1)], X1 + j)
        parts = [
            jnp.concatenate(
                [x1_recv[j, :, part, c].reshape(plane, width) for c in range(cycles)], axis=0
            )
            for part in range(2)
        ]
        values = jnp.concatenate(parts, axis=1)
        found = jnp.dot(leg[j], values, preferred_element_type=F32)
        weight = jnp.where(rank * modes + j == 0, 1.0, 2.0).astype(F32)
        scale = gain * weight
        scaled = (found * jnp.concatenate([scale, scale], axis=1)).astype(BF16)
        back = jnp.dot(leg_t[j], scaled, preferred_element_type=F32).astype(BF16)
        for part in range(2):
            piece = back[:plane, part * width : (part + 1) * width]
            x2_send[j, :, 0, part] = piece.reshape(Q, Z, width)
        send_rows(j, pl.ds(0, 1), X2)
        x2_recv[j, q, 0] = x2_send[j, q, 0]
        gathered[j, y] = back[plane:]

        @pl.loop(1, Y)
        def _(i):
            send(gathered.at[j, y], gathered.at[j, y], GATHER + j, {"chan": lax.rem(y + i, Y)})

    def mix(j):
        await_recv(gathered.at[j, pl.ds(0, Y - 1)], GATHER + j)
        values = jnp.concatenate([gathered[j, a] for a in range(Y)], axis=1)
        mixed = jnp.dot(values, mix_w[...], preferred_element_type=F32).astype(BF16)
        for c in range(1, cycles):
            for part in range(2):
                piece = mixed[(c - 1) * plane : c * plane, part * width : (part + 1) * width]
                x2_send[j, :, c, part] = piece.reshape(Q, Z, width)
        send_rows(j, rest, X2_REST)
        x2_recv[j, q, 1:] = x2_send[j, q, 1:]

    def to_cycles(j, which):
        if which == [0]:
            await_recv(x2_recv.at[j, pl.ds(0, Q - 1), 0], X2 + j)
        else:
            await_recv(x2_recv.at[j, pl.ds(0, Q - 1), rest], X2_REST + j)
        for c in which:
            parts = [x2_recv[j, a, c, part].astype(F32) for part in range(2) for a in range(Q)]
            z2_send[j, :, c] = jnp.swapaxes(jnp.stack(parts), 0, 1).astype(BF16)

            @pl.loop(0, Z - 1)
            def _(i):
                other = ring_place(i)
                send(
                    z2_send.at[j, other, c],
                    z2_recv.at[j, z, c],
                    (LAST if j == last else EARLY) + c,
                    {"lat_1": other},
                )

            z2_recv[j, z, c] = z2_send[j, z, c]

    def place(at, values):
        padded[at, pad : pad + nlon] = values
        padded[at, 0:pad] = values[nlon - pad :]
        padded[at, pad + nlon :] = values[:pad]

    def pad_field():
        for c in range(cycles):
            place(c + 1, grid_v[c].astype(F32))

        @pl.when(rank > 0)
        def _():
            await_recv(halo.at[0], BEFORE)
            place(0, halo[0].astype(F32))

        @pl.when(rank == 0)
        def _():
            padded[0] = jnp.zeros(padded.shape[1:], F32)

        @pl.when(rank < R - 1)
        def _():
            await_recv(halo.at[1], AFTER)
            place(cycles + 1, halo[1].astype(F32))

        @pl.when(rank == R - 1)
        def _():
            padded[cycles + 1] = jnp.zeros(padded.shape[1:], F32)

    def sine(cycle):
        angle = jnp.full((1, width), cycle, jnp.int32).astype(F32)
        return jnp.sin(math.pi * (angle + 0.5) / (R * cycles))

    def local_field(c):
        taps = conv_in.shape[0]
        block = 5 * TILE if nlon % (5 * TILE) == 0 else TILE
        own = rank * cycles + c
        here = sine(own)
        weights = [
            conv_in[tap : tap + 1, :] * (sine(own + lat_off[tap]) / here) for tap in range(taps)
        ]

        @pl.loop(0, nlon // block)
        def _(b):
            first = pl.multiple_of(b * block, TILE)
            total = padded[c + 1, pl.ds(pad + first, block), :]
            for tap in range(taps):
                source = padded[c + 1 + lat_off[tap], pl.ds(pad + first + lon_off[tap], block), :]
                total = total + weights[tap] * source
            if c == 0:
                local_send[pl.ds(first, block), :] = total.astype(BF16)
            else:
                base[c - 1, pl.ds(first, block), :] = total

    mine = pl.multiple_of(y * step, TILE)

    def share(src, dst, at):
        @pl.loop(1, Y)
        def _(i):
            other = lax.rem(y + i, Y)
            first = pl.multiple_of(other * step, TILE)
            part = (slice(None),) * (len(src.shape) - 2) + (pl.ds(first, size),)
            send(src.at[part], dst.at[y], at, {"chan": other})

    def share_local():
        pad_field()
        for c in range(cycles):
            local_field(c)
        share(local_send, local_recv, LOCAL)
        local_recv[y] = local_send[pl.ds(mine, size)]

    later = list(range(1, cycles))
    to_owners(0)
    legendre(0)
    for j in range(1, modes):
        to_owners(j)
        to_cycles(j - 1, [0])
        if j > 1:
            to_cycles(j - 2, later)
        legendre(j)
        mix(j - 1)
    share_local()
    to_cycles(last, [0])
    if last > 0:
        to_cycles(last - 1, later)
    mix(last)
    for i in range(3):
        copies[REST + i].wait()
    to_cycles(last, later)
    await_recv(mix_all.at[pl.ds(0, Y - 1)], MIX)
    await_recv(local_recv.at[pl.ds(0, Y - 1)], LOCAL)

    def both_parts(value):
        wide = value.astype(F32)
        turned = jnp.concatenate([-wide[:, Q:], wide[:, :Q]], axis=1).astype(BF16)
        return [value.reshape(2 * R, width), turned.reshape(2 * R, width)]

    def to_points(c):
        def values(j):
            value = z2_recv[j, :, c]
            if c == 0:
                return jnp.concatenate(both_parts(value), axis=1)
            return value.reshape(2 * R, width)

        await_recv(z2_recv.at[early, pl.ds(0, Z - 1), c], EARLY + c)
        found = base[c - 1] if c > 0 else None
        for j in range(modes):
            if j == last:
                await_recv(z2_recv.at[last, pl.ds(0, Z - 1), c], LAST + c)
            term = jnp.dot(inverse[j], values(j), preferred_element_type=F32)
            found = term if found is None else found + term
        if c == 0:
            fields = found.astype(BF16)
            field_send[0] = fields[:, :width]
            field_send[1] = fields[:, width:]
            share(field_send, field_recv, FIELD)
            field_recv[y] = field_send[:, pl.ds(mine, size)]
        else:
            sum_send[c - 1] = found.astype(BF16)
            share(sum_send.at[c - 1], sum_recv.at[c - 1], FIELD + c)
            sum_recv[c - 1, y] = sum_send[c - 1, pl.ds(mine, size)]

    def perceptron(c):
        if c == 0:
            await_recv(field_recv.at[pl.ds(0, Y - 1)], FIELD)
            points = jnp.concatenate(
                [field_recv[a, part] for part in range(2) for a in range(Y)], axis=1
            )
            pieces = []
            for a in range(Y):
                weights = jnp.concatenate([mix_all[a, 0], mix_all[a, 1]], axis=0)
                pieces.append(jnp.dot(points, weights, preferred_element_type=F32))
            near = jnp.concatenate([local_recv[a] for a in range(Y)], axis=1)
            row = (jnp.concatenate(pieces, axis=1) + near.astype(F32)).astype(BF16)
        else:
            await_recv(sum_recv.at[c - 1, pl.ds(0, Y - 1)], FIELD + c)
            row = jnp.concatenate([sum_recv[c - 1, a] for a in range(Y)], axis=1)
        row = row.astype(F32)
        center = jnp.mean(row, axis=-1, keepdims=True)
        off = row - center
        spread = jnp.mean(off * off, axis=-1, keepdims=True)
        normed = (off / jnp.sqrt(spread + 1e-05) * norm_in[...]).astype(BF16)
        hidden = jax.nn.gelu(
            jnp.dot(normed, up_w[...], preferred_element_type=F32), approximate=True
        ).astype(BF16)
        result = (jnp.dot(hidden, down_w[...], preferred_element_type=F32) + row).astype(BF16)
        for a in range(Y):
            out_send[c, a] = result[:, a * width : (a + 1) * width]

        @pl.loop(1, Y)
        def _(i):
            other = lax.rem(y + i, Y)
            send(
                out_send.at[c, other, pl.ds(0, step)],
                out.at[c, pl.ds(mine, step)],
                OUT + c,
                {"chan": other},
            )

            @pl.when(y == Y - 1)
            def _():
                send(
                    out_send.at[c, other, pl.ds(step, size - step)],
                    out.at[c, pl.ds(Y * step, size - step)],
                    EXTRA + c,
                    {"chan": other},
                )

        out[c, pl.ds(mine, step), :] = out_send[c, y, 0:step]

        @pl.when(y == Y - 1)
        def _():
            out[c, Y * step :, :] = out_send[c, y, step:]

    def finish(c):
        await_recv(out.at[c, pl.ds(0, (Y - 1) * step)], OUT + c)

        @pl.when(y < Y - 1)
        def _():
            await_recv(out.at[c, pl.ds(0, size - step)], EXTRA + c)


    to_points(0)
    for c in range(1, cycles):
        to_points(c)
        perceptron(c - 1)
    perceptron(cycles - 1)
    for c in range(cycles):
        finish(c)

    for j in range(modes):
        await_send(z1_send.at[j, pl.ds(0, Z - 1)], Z1 + j)
        await_send(x1_send.at[j, pl.ds(0, Q - 1)], X1 + j)
        await_send(x2_send.at[j, pl.ds(0, Q - 1), 0], X2 + j)
        await_send(x2_send.at[j, pl.ds(0, Q - 1), rest], X2_REST + j)
        await_send(gathered.at[j, pl.ds(0, Y - 1)], GATHER + j)
    await_send(local_recv.at[pl.ds(0, Y - 1)], LOCAL)
    await_send(mix_all.at[pl.ds(0, Y - 1)], MIX)
    for c in range(cycles):
        await_send(z2_send.at[early, pl.ds(0, Z - 1), c], EARLY + c)
        await_send(z2_send.at[last, pl.ds(0, Z - 1), c], LAST + c)
        if c == 0:
            await_send(field_recv.at[pl.ds(0, Y - 1)], FIELD)
        else:
            await_send(sum_recv.at[c - 1, pl.ds(0, Y - 1)], FIELD + c)
        await_send(out.at[c, pl.ds(0, (Y - 1) * step)], OUT + c)

        @pl.when(y == Y - 1)
        def _():
            await_send(out.at[c, pl.ds(0, (Y - 1) * (size - step))], EXTRA + c)

    @pl.when(rank < R - 1)
    def _():
        await_send(halo.at[0], BEFORE)

    @pl.when(rank > 0)
    def _():
        await_send(halo.at[1], AFTER)


def on_device(
    sizes,
    grid,
    basis,
    mix_weight,
    spectral_gain,
    conv_weight,
    lat_offsets,
    lon_offsets,
    ln_gain,
    up_weight,
    down_weight,
):
    X, Z, K, Y = sizes
    cycles, nlon, width = grid.shape
    modes, L, nlat = basis.shape
    C = width * Y
    Q = X * K
    step = nlon // (Y * TILE) * TILE
    size = nlon - (Y - 1) * step
    table = transform_tables(X, Z, K, modes, nlon)
    inverse = np.ascontiguousarray(table.transpose(0, 2, 1))
    perm = np.zeros((nlat, nlat), ml_dtypes.bfloat16)
    perm[np.arange(nlat), cycle_order(X, Z, K, cycles)] = 1
    theta = (math.pi * (np.arange(nlat, dtype=np.float32) + np.float32(0.5)) / nlat).astype(
        np.float32
    )
    quad = (np.float32(math.pi / nlat) * np.sin(theta)).astype(np.float32)[None, :]
    dims = (X, Z, K, Y, cycles, modes, L, nlon, width, step, size)
    any_space = pl.BlockSpec(memory_space=pl.ANY)
    vmem = pl.BlockSpec(memory_space=pltpu.VMEM)
    smem = pl.BlockSpec(memory_space=pltpu.SMEM)
    pad = 8
    n_sem = 5 * modes + 5 * cycles + 4
    around_z = (modes, Z, cycles, 2 * Q, width)
    around_q = (modes, Q, 2, cycles, Z, width)
    around_back = (modes, Q, cycles, 2, Z, width)
    scratch = [
        pltpu.VMEM((cycles, nlon, width), BF16),
        pltpu.VMEM(table.shape, BF16),
        pltpu.VMEM(inverse.shape, BF16),
        pltpu.VMEM(perm.shape, BF16),
        pltpu.VMEM(basis.shape, F32),
        pltpu.VMEM((Y, 2, C, width), BF16),
        pltpu.VMEM((2 * C, 2 * width), BF16),
        pltpu.VMEM(up_weight.shape, BF16),
        pltpu.VMEM(down_weight.shape, BF16),
        pltpu.VMEM((modes, L, nlat), BF16),
        pltpu.VMEM((modes, nlat, L), BF16),
        pltpu.VMEM(around_z, BF16),
        pltpu.VMEM(around_z, BF16),
        pltpu.VMEM(around_q, BF16),
        pltpu.VMEM(around_q, BF16),
        pltpu.VMEM((modes, Y, (cycles - 1) * Q * Z, 2 * width), BF16),
        pltpu.VMEM(around_back, BF16),
        pltpu.VMEM(around_back, BF16),
        pltpu.VMEM(around_z, BF16),
        pltpu.VMEM(around_z, BF16),
        pltpu.VMEM((2, nlon, width), BF16),
        pltpu.VMEM((cycles + 2, nlon + 2 * pad, width), F32),
        pltpu.VMEM((cycles - 1, nlon, width), F32),
        pltpu.VMEM((nlon, width), BF16),
        pltpu.VMEM((Y, size, width), BF16),
        pltpu.VMEM((2, nlon, width), BF16),
        pltpu.VMEM((Y, 2, size, width), BF16),
        pltpu.VMEM((cycles - 1, nlon, width), BF16),
        pltpu.VMEM((cycles - 1, Y, size, width), BF16),
        pltpu.VMEM((cycles, Y, size, width), BF16),
        pltpu.SemaphoreType.DMA((7 + modes,)),
        pltpu.SemaphoreType.DMA((n_sem,)),
        pltpu.SemaphoreType.DMA((n_sem,)),
    ]
    return pl.pallas_call(
        functools.partial(block_kernel, dims),
        out_shape=pltpu.VMEM(grid.shape, BF16),
        in_specs=[any_space] * 6
        + [vmem, vmem, vmem, smem, smem, vmem]
        + [any_space] * 2,
        out_specs=vmem,
        scratch_shapes=scratch,
        compiler_params=pltpu.CompilerParams(
            collective_id=0, has_side_effects=True, vmem_limit_bytes=56 * 1024 * 1024
        ),
        name="block",
    )(
        grid,
        jnp.asarray(table),
        jnp.asarray(inverse),
        jnp.asarray(perm),
        basis,
        mix_weight,
        spectral_gain,
        jnp.asarray(quad),
        conv_weight,
        lat_offsets,
        lon_offsets,
        ln_gain.reshape(1, C),
        up_weight,
        down_weight,
    )


def build(finer):
    sizes = tuple(finer.shape[a] for a in (*LAT, "chan"))
    return jax.shard_map(
        functools.partial(on_device, sizes),
        mesh=finer,
        in_specs=(
            P(LAT, None, "chan"),
            P(LAT, None, None),
            P(None, None, "chan"),
            P(),
            P(None, "chan"),
            P(),
            P(),
            P(),
            P(),
            P(),
        ),
        out_specs=P(LAT, None, "chan"),
        check_vma=False,
    )


def solution(mesh):
    return build(
        Mesh(mesh.devices.reshape(4, 16, 2, mesh.shape["chan"]), (*LAT, "chan"))
    )
```

```python
import functools
import math

import jax
import jax.numpy as jnp
import ml_dtypes
import numpy as np
from jax import lax
from jax.experimental import pallas as pl
from jax.experimental.pallas import tpu as pltpu
from jax.sharding import Mesh
from jax.sharding import PartitionSpec as P

LAT = ("lat_0", "lat_1", "lat_2")
MESH_ID = pl.DeviceIdType.MESH
TILE = 16
F32 = jnp.float32
BF16 = jnp.bfloat16


def transform_tables(X, Z, K, modes, nlon):
    j, z, ri, x, k = np.meshgrid(
        np.arange(modes), np.arange(Z), np.arange(2), np.arange(X), np.arange(K), indexing="ij"
    )
    m = (((x * Z + z) * K + k) * modes + j).reshape(modes, -1).astype(np.int64)
    part = ri.reshape(modes, -1)
    points = np.arange(nlon, dtype=np.int64)
    phase = (m[:, :, None] * points) % nlon
    angle = np.float32(2.0 * math.pi) * phase.astype(np.float32) / np.float32(nlon)
    table = np.where(part[:, :, None] == 0, np.cos(angle), -np.sin(angle)).astype(np.float32)
    return table.astype(ml_dtypes.bfloat16)


def cycle_order(X, Z, K, cycles):
    c, x, k, z = np.meshgrid(
        np.arange(cycles), np.arange(X), np.arange(K), np.arange(Z), indexing="ij"
    )
    return (((x * Z + z) * K + k) * cycles + c).reshape(-1)


def block_kernel(
    dims,
    grid_in,
    table_in,
    inverse_in,
    perm_in,
    basis_in,
    mix_in,
    gain_hbm,
    quad_hbm,
    conv_hbm,
    lat_hbm,
    lon_hbm,
    norm_hbm,
    up_in,
    down_in,
    out,
    gain_in,
    quad_in,
    conv_in,
    lat_off,
    lon_off,
    norm_in,
    grid_v,
    table,
    inverse,
    perm,
    basis,
    mix_all,
    mix_w,
    up_w,
    down_w,
    leg,
    leg_t,
    z1_send,
    z1_recv,
    x1_send,
    x1_recv,
    gathered,
    x2_send,
    x2_recv,
    z2_send,
    z2_recv,
    halo,
    padded,
    base,
    fields0,
    local_send,
    local_recv,
    field_send,
    field_recv,
    sum_send,
    sum_recv,
    out_send,
    load_sem,
    send_sem,
    recv_sem,
):
    X, Z, K, Y, cycles, modes, L, nlon, width, step, size = dims
    Q = X * K
    R = Q * Z
    x = lax.axis_index("lat_0")
    z = lax.axis_index("lat_1")
    k = lax.axis_index("lat_2")
    y = lax.axis_index("chan")
    q = x * K + k
    rank = (x * Z + z) * K + k
    last = modes - 1
    early = pl.ds(0, last)
    rest = pl.ds(1, cycles - 1)
    plane = Q * Z
    pad = (padded.shape[1] - nlon) // 2

    loads = [(table_in.at[0], table.at[0]), (grid_in, grid_v)]
    loads += [(table_in.at[j], table.at[j]) for j in range(1, modes)]
    BASIS = len(loads)
    loads += [(basis_in, basis), (perm_in, perm), (mix_in, mix_all.at[y])]
    loads += [(gain_hbm, gain_in), (quad_hbm, quad_in)]
    REST = len(loads)
    loads += [(inverse_in, inverse), (up_in, up_w), (down_in, down_w)]
    loads += [(conv_hbm, conv_in), (lat_hbm, lat_off), (lon_hbm, lon_off), (norm_hbm, norm_in)]
    copies = [
        pltpu.make_async_copy(src, dst, load_sem.at[i]) for i, (src, dst) in enumerate(loads)
    ]
    def q_device(other):
        return {"lat_0": other // K, "lat_2": lax.rem(other, K)}

    def rank_device(r):
        return {"lat_0": r // (Z * K), "lat_1": lax.rem(r // K, Z), "lat_2": lax.rem(r, K)}

    barrier = pltpu.get_barrier_semaphore()

    def greet(device):
        pl.semaphore_signal(barrier, inc=1, device_id=device, device_id_type=MESH_ID)

    def ring_place(i):
        far = Z - 1 - i
        offset = jnp.where(lax.rem(far, 2) == 1, (far + 1) // 2, Z - far // 2)
        return lax.rem(z + offset, Z)

    @pl.loop(0, Z - 1)
    def _(i):
        greet({"lat_1": ring_place(i)})

    copies[0].start()
    copies[1].start()

    @pl.loop(1, Q)
    def _(i):
        greet(q_device(lax.rem(q + i, Q)))

    @pl.loop(1, Y)
    def _(i):
        greet({"chan": lax.rem(y + i, Y)})

    @pl.when(rank > 0)
    def _():
        greet(rank_device(rank - 1))

    @pl.when(rank < R - 1)
    def _():
        greet(rank_device(rank + 1))

    def send(src, dst, at, device):
        pltpu.make_async_remote_copy(
            src_ref=src,
            dst_ref=dst,
            send_sem=send_sem.at[at],
            recv_sem=recv_sem.at[at],
            device_id=device,
            device_id_type=MESH_ID,
        ).start()

    def await_recv(ref, at):
        pltpu.make_async_copy(ref, ref, recv_sem.at[at]).wait()

    def await_send(ref, at):
        pltpu.make_async_copy(ref, ref, send_sem.at[at]).wait()

    Z1, X1, X2, X2_REST, GATHER = (n * modes for n in range(5))
    EARLY = 5 * modes
    LAST = EARLY + cycles
    FIELD = LAST + cycles
    OUT = FIELD + cycles
    EXTRA = OUT + cycles
    LOCAL = EXTRA + cycles
    MIX = LOCAL + 1
    BEFORE = LOCAL + 2
    AFTER = LOCAL + 3
    FIELD_TAIL = LOCAL + 4
    OUT_TAIL = LOCAL + 5
    cut = size // 2 // TILE * TILE

    def forward(j):
        points = jnp.concatenate([grid_v[c] for c in range(cycles)], axis=1)
        spec = jnp.dot(table[j], points, preferred_element_type=F32) * (1.0 / nlon)
        spec = spec.astype(BF16)
        for c in range(cycles):
            z1_send[j, :, c] = spec[:, c * width : (c + 1) * width].reshape(Z, 2 * Q, width)

    def send_z(buf, land, j, at):
        @pl.loop(0, Z - 1)
        def _(i):
            other = ring_place(i)
            send(buf.at[j, other], land.at[j, z], at + j, {"lat_1": other})

        land[j, z] = buf[j, z]

    def send_q(buf, land, j, at):
        @pl.loop(1, Q)
        def _(i):
            other = lax.rem(q + i, Q)
            send(buf.at[j, other], land.at[j, q], at + j, q_device(other))

        land[j, q] = buf[j, q]

    copies[0].wait()
    copies[1].wait()
    for copy in copies[2:]:
        copy.start()
    forward(0)
    greeted = (Z - 1) + (Q - 1) + (Y - 1)
    greeted = greeted + jnp.where(rank > 0, 1, 0) + jnp.where(rank < R - 1, 1, 0)
    pl.semaphore_wait(barrier, greeted)
    send_z(z1_send, z1_recv, 0, Z1)

    for j in range(1, modes):
        copies[1 + j].wait()
        forward(j)
        send_z(z1_send, z1_recv, j, Z1)

    @pl.when(rank < R - 1)
    def _():
        send(grid_v.at[cycles - 1], halo.at[0], BEFORE, rank_device(rank + 1))

    @pl.when(rank > 0)
    def _():
        send(grid_v.at[0], halo.at[1], AFTER, rank_device(rank - 1))

    copies[BASIS].wait()
    copies[BASIS + 1].wait()
    copies[BASIS + 2].wait()
    copies[BASIS + 3].wait()
    copies[BASIS + 4].wait()

    @pl.loop(1, Y)
    def _(i):
        send(mix_all.at[y], mix_all.at[y], MIX, {"chan": lax.rem(y + i, Y)})

    for j in range(modes):
        weighted = (basis[j] * quad_in[...]).astype(BF16)
        leg[j] = lax.dot_general(
            weighted, perm[...], (((1,), (1,)), ((), ())), preferred_element_type=F32
        ).astype(BF16)
        leg_t[j] = lax.dot_general(
            perm[...], basis[j].astype(BF16), (((1,), (1,)), ((), ())), preferred_element_type=F32
        ).astype(BF16)
    for a in range(Y):
        real = mix_all[y, 0, a * width : (a + 1) * width, :]
        imag = mix_all[y, 1, a * width : (a + 1) * width, :]
        at = 2 * a * width
        mix_w[at : at + width, :width] = real
        mix_w[at : at + width, width:] = imag
        mix_w[at + width : at + 2 * width, :width] = -imag
        mix_w[at + width : at + 2 * width, width:] = real
    gain = jnp.transpose(jnp.broadcast_to(gain_in[...].reshape(1, L), (width, L)))

    def to_owners(j):
        await_recv(z1_recv.at[j, pl.ds(0, Z - 1)], Z1 + j)
        for c in range(cycles):
            turned = jnp.swapaxes(z1_recv[j, :, c].astype(F32), 0, 1).astype(BF16)
            for part in range(2):
                x1_send[j, :, part, c] = turned[part * Q : (part + 1) * Q]
        send_q(x1_send, x1_recv, j, X1)

    def send_rows(j, cut, at):
        @pl.loop(1, Q)
        def _(i):
            other = lax.rem(q + i, Q)
            send(x2_send.at[j, other, cut], x2_recv.at[j, q, cut], at + j, q_device(other))

    def legendre(j):
        await_recv(x1_recv.at[j, pl.ds(0, Q - 1)], X1 + j)
        parts = [
            jnp.concatenate(
                [x1_recv[j, :, part, c].reshape(plane, width) for c in range(cycles)], axis=0
            )
            for part in range(2)
        ]
        values = jnp.concatenate(parts, axis=1)
        found = jnp.dot(leg[j], values, preferred_element_type=F32)
        weight = jnp.where(rank * modes + j == 0, 1.0, 2.0).astype(F32)
        scale = gain * weight
        scaled = (found * jnp.concatenate([scale, scale], axis=1)).astype(BF16)
        back = jnp.dot(leg_t[j], scaled, preferred_element_type=F32).astype(BF16)
        for part in range(2):
            piece = back[:plane, part * width : (part + 1) * width]
            x2_send[j, :, 0, part] = piece.reshape(Q, Z, width)
        send_rows(j, pl.ds(0, 1), X2)
        x2_recv[j, q, 0] = x2_send[j, q, 0]
        gathered[j, y] = back[plane:]

        @pl.loop(1, Y)
        def _(i):
            send(gathered.at[j, y], gathered.at[j, y], GATHER + j, {"chan": lax.rem(y + i, Y)})

    def mix(j):
        await_recv(gathered.at[j, pl.ds(0, Y - 1)], GATHER + j)
        values = jnp.concatenate([gathered[j, a] for a in range(Y)], axis=1)
        mixed = jnp.dot(values, mix_w[...], preferred_element_type=F32).astype(BF16)
        for c in range(1, cycles):
            for part in range(2):
                piece = mixed[(c - 1) * plane : c * plane, part * width : (part + 1) * width]
                x2_send[j, :, c, part] = piece.reshape(Q, Z, width)
        send_rows(j, rest, X2_REST)
        x2_recv[j, q, 1:] = x2_send[j, q, 1:]

    def to_cycles(j, which):
        if which == [0]:
            await_recv(x2_recv.at[j, pl.ds(0, Q - 1), 0], X2 + j)
        else:
            await_recv(x2_recv.at[j, pl.ds(0, Q - 1), rest], X2_REST + j)
        for c in which:
            parts = [x2_recv[j, a, c, part].astype(F32) for part in range(2) for a in range(Q)]
            z2_send[j, :, c] = jnp.swapaxes(jnp.stack(parts), 0, 1).astype(BF16)

            @pl.loop(0, Z - 1)
            def _(i):
                other = ring_place(i)
                send(
                    z2_send.at[j, other, c],
                    z2_recv.at[j, z, c],
                    (LAST if j == last else EARLY) + c,
                    {"lat_1": other},
                )

            z2_recv[j, z, c] = z2_send[j, z, c]

    def place(at, values):
        padded[at, pad : pad + nlon] = values
        padded[at, 0:pad] = values[nlon - pad :]
        padded[at, pad + nlon :] = values[:pad]

    def pad_field():
        for c in range(cycles):
            place(c + 1, grid_v[c].astype(F32))

        @pl.when(rank > 0)
        def _():
            await_recv(halo.at[0], BEFORE)
            place(0, halo[0].astype(F32))

        @pl.when(rank == 0)
        def _():
            padded[0] = jnp.zeros(padded.shape[1:], F32)

        @pl.when(rank < R - 1)
        def _():
            await_recv(halo.at[1], AFTER)
            place(cycles + 1, halo[1].astype(F32))

        @pl.when(rank == R - 1)
        def _():
            padded[cycles + 1] = jnp.zeros(padded.shape[1:], F32)

    def sine(cycle):
        angle = jnp.full((1, width), cycle, jnp.int32).astype(F32)
        return jnp.sin(math.pi * (angle + 0.5) / (R * cycles))

    def local_field(c):
        taps = conv_in.shape[0]
        block = 5 * TILE if nlon % (5 * TILE) == 0 else TILE
        own = rank * cycles + c
        here = sine(own)
        weights = [
            conv_in[tap : tap + 1, :] * (sine(own + lat_off[tap]) / here) for tap in range(taps)
        ]

        @pl.loop(0, nlon // block)
        def _(b):
            first = pl.multiple_of(b * block, TILE)
            total = padded[c + 1, pl.ds(pad + first, block), :]
            for tap in range(taps):
                source = padded[c + 1 + lat_off[tap], pl.ds(pad + first + lon_off[tap], block), :]
                total = total + weights[tap] * source
            if c == 0:
                local_send[pl.ds(first, block), :] = total.astype(BF16)
            else:
                base[c - 1, pl.ds(first, block), :] = total

    mine = pl.multiple_of(y * step, TILE)

    def share(src, dst, at, low=0, rows=None):
        rows = size if rows is None else rows

        @pl.loop(1, Y)
        def _(i):
            other = lax.rem(y + i, Y)
            first = pl.multiple_of(other * step, TILE) + low
            lead = (slice(None),) * (len(src.shape) - 2)
            send(
                src.at[(*lead, pl.ds(first, rows))],
                dst.at[(y, *lead, pl.ds(low, rows))],
                at,
                {"chan": other},
            )

    def share_local():
        pad_field()
        for c in range(cycles):
            local_field(c)
        share(local_send, local_recv, LOCAL)
        local_recv[y] = local_send[pl.ds(mine, size)]

    later = list(range(1, cycles))
    to_owners(0)
    legendre(0)
    for j in range(1, modes):
        to_owners(j)
        to_cycles(j - 1, [0])
        if j > 1:
            to_cycles(j - 2, later)
        legendre(j)
        mix(j - 1)
    for copy in copies[REST:]:
        copy.wait()
    share_local()
    to_cycles(last, [0])
    if last > 0:
        to_cycles(last - 1, later)
    def both_parts(value):
        wide = value.astype(F32)
        turned = jnp.concatenate([-wide[:, Q:], wide[:, :Q]], axis=1).astype(BF16)
        return [value.reshape(2 * R, width), turned.reshape(2 * R, width)]

    def values_of(j, c):
        value = z2_recv[j, :, c]
        if c == 0:
            return jnp.concatenate(both_parts(value), axis=1)
        return value.reshape(2 * R, width)

    def partly(c):
        await_recv(z2_recv.at[early, pl.ds(0, Z - 1), c], EARLY + c)
        found = base[c - 1] if c > 0 else None
        for j in range(last):
            term = jnp.dot(inverse[j], values_of(j, c), preferred_element_type=F32)
            found = term if found is None else found + term
        if c == 0:
            fields0[...] = found
        else:
            base[c - 1] = found

    def to_points(c):
        await_recv(z2_recv.at[last, pl.ds(0, Z - 1), c], LAST + c)
        found = fields0[...] if c == 0 else base[c - 1]
        found = found + jnp.dot(inverse[last], values_of(last, c), preferred_element_type=F32)
        if c == 0:
            fields = found.astype(BF16)
            field_send[0] = fields[:, :width]
            field_send[1] = fields[:, width:]
            share(field_send, field_recv, FIELD)
            field_recv[y] = field_send[:, pl.ds(mine, size)]
        else:
            sum_send[c - 1] = found.astype(BF16)
            if c == cycles - 1:
                share(sum_send.at[c - 1], sum_recv.at[c - 1], FIELD + c, 0, cut)
                share(sum_send.at[c - 1], sum_recv.at[c - 1], FIELD_TAIL, cut, size - cut)
            else:
                share(sum_send.at[c - 1], sum_recv.at[c - 1], FIELD + c)
            sum_recv[c - 1, y] = sum_send[c - 1, pl.ds(mine, size)]

    def perceptron(c, low=0, rows=None):
        rows = size if rows is None else rows
        own = slice(low, low + rows)
        out_at, field_at = (OUT + c, FIELD + c) if low == 0 else (OUT_TAIL, FIELD_TAIL)
        if c == 0:
            await_recv(field_recv.at[pl.ds(0, Y - 1)], FIELD)
            points = jnp.concatenate(
                [field_recv[a, part] for part in range(2) for a in range(Y)], axis=1
            )
            pieces = []
            for a in range(Y):
                weights = jnp.concatenate([mix_all[a, 0], mix_all[a, 1]], axis=0)
                pieces.append(jnp.dot(points, weights, preferred_element_type=F32))
            near = jnp.concatenate([local_recv[a] for a in range(Y)], axis=1)
            row = (jnp.concatenate(pieces, axis=1) + near.astype(F32)).astype(BF16)
        else:
            await_recv(sum_recv.at[c - 1, pl.ds(0, Y - 1), pl.ds(low, rows)], field_at)
            row = jnp.concatenate([sum_recv[c - 1, a, own] for a in range(Y)], axis=1)
        row = row.astype(F32)
        center = jnp.mean(row, axis=-1, keepdims=True)
        off = row - center
        spread = jnp.mean(off * off, axis=-1, keepdims=True)
        normed = (off / jnp.sqrt(spread + 1e-05) * norm_in[...]).astype(BF16)
        hidden = jax.nn.gelu(
            jnp.dot(normed, up_w[...], preferred_element_type=F32), approximate=True
        ).astype(BF16)
        result = (jnp.dot(hidden, down_w[...], preferred_element_type=F32) + row).astype(BF16)
        for a in range(Y):
            out_send[c, a, own] = result[:, a * width : (a + 1) * width]
        main = min(low + rows, step) - low
        extra = low + rows > step

        @pl.loop(1, Y)
        def _(i):
            other = lax.rem(y + i, Y)
            send(
                out_send.at[c, other, pl.ds(low, main)],
                out.at[c, pl.ds(mine + low, main)],
                out_at,
                {"chan": other},
            )

            if extra:

                @pl.when(y == Y - 1)
                def _():
                    send(
                        out_send.at[c, other, pl.ds(step, size - step)],
                        out.at[c, pl.ds(Y * step, size - step)],
                        EXTRA + c,
                        {"chan": other},
                    )

        out[c, pl.ds(mine + low, main), :] = out_send[c, y, low : low + main]

        if extra:

            @pl.when(y == Y - 1)
            def _():
                out[c, Y * step :, :] = out_send[c, y, step:]

    def out_pieces(c):
        if c < cycles - 1:
            return [(OUT + c, step)]
        return [(OUT + c, cut), (OUT_TAIL, step - cut)]

    def finish(c):
        for at, main in out_pieces(c):
            await_recv(out.at[c, pl.ds(0, (Y - 1) * main)], at)

        @pl.when(y < Y - 1)
        def _():
            await_recv(out.at[c, pl.ds(0, size - step)], EXTRA + c)


    partly(0)
    mix(last)
    to_points(0)
    to_cycles(last, later)
    partly(1)
    await_recv(mix_all.at[pl.ds(0, Y - 1)], MIX)
    await_recv(local_recv.at[pl.ds(0, Y - 1)], LOCAL)
    perceptron(0)
    for c in range(1, cycles):
        if c > 1:
            partly(c)
        to_points(c)
    for c in range(1, cycles - 1):
        perceptron(c)
    perceptron(cycles - 1, 0, cut)
    perceptron(cycles - 1, cut, size - cut)
    for c in range(cycles):
        finish(c)

    for j in range(modes):
        await_send(z1_send.at[j, pl.ds(0, Z - 1)], Z1 + j)
        await_send(x1_send.at[j, pl.ds(0, Q - 1)], X1 + j)
        await_send(x2_send.at[j, pl.ds(0, Q - 1), 0], X2 + j)
        await_send(x2_send.at[j, pl.ds(0, Q - 1), rest], X2_REST + j)
        await_send(gathered.at[j, pl.ds(0, Y - 1)], GATHER + j)
    await_send(local_recv.at[pl.ds(0, Y - 1)], LOCAL)
    await_send(mix_all.at[pl.ds(0, Y - 1)], MIX)
    for c in range(cycles):
        await_send(z2_send.at[early, pl.ds(0, Z - 1), c], EARLY + c)
        await_send(z2_send.at[last, pl.ds(0, Z - 1), c], LAST + c)
        if c == 0:
            await_send(field_recv.at[pl.ds(0, Y - 1)], FIELD)
        elif c < cycles - 1:
            await_send(sum_recv.at[c - 1, pl.ds(0, Y - 1)], FIELD + c)
        else:
            await_send(sum_recv.at[c - 1, pl.ds(0, Y - 1), pl.ds(0, cut)], FIELD + c)
            await_send(sum_recv.at[c - 1, pl.ds(0, Y - 1), pl.ds(cut, size - cut)], FIELD_TAIL)
        for at, main in out_pieces(c):
            await_send(out.at[c, pl.ds(0, (Y - 1) * main)], at)

        @pl.when(y == Y - 1)
        def _():
            await_send(out.at[c, pl.ds(0, (Y - 1) * (size - step))], EXTRA + c)

    @pl.when(rank < R - 1)
    def _():
        await_send(halo.at[0], BEFORE)

    @pl.when(rank > 0)
    def _():
        await_send(halo.at[1], AFTER)


def on_device(
    sizes,
    grid,
    basis,
    mix_weight,
    spectral_gain,
    conv_weight,
    lat_offsets,
    lon_offsets,
    ln_gain,
    up_weight,
    down_weight,
):
    X, Z, K, Y = sizes
    cycles, nlon, width = grid.shape
    modes, L, nlat = basis.shape
    C = width * Y
    Q = X * K
    step = nlon // (Y * TILE) * TILE
    size = nlon - (Y - 1) * step
    table = transform_tables(X, Z, K, modes, nlon)
    inverse = np.ascontiguousarray(table.transpose(0, 2, 1))
    perm = np.zeros((nlat, nlat), ml_dtypes.bfloat16)
    perm[np.arange(nlat), cycle_order(X, Z, K, cycles)] = 1
    theta = (math.pi * (np.arange(nlat, dtype=np.float32) + np.float32(0.5)) / nlat).astype(
        np.float32
    )
    quad = (np.float32(math.pi / nlat) * np.sin(theta)).astype(np.float32)[None, :]
    dims = (X, Z, K, Y, cycles, modes, L, nlon, width, step, size)
    any_space = pl.BlockSpec(memory_space=pl.ANY)
    vmem = pl.BlockSpec(memory_space=pltpu.VMEM)
    pad = 8
    n_sem = 5 * modes + 5 * cycles + 6
    around_z = (modes, Z, cycles, 2 * Q, width)
    around_q = (modes, Q, 2, cycles, Z, width)
    around_back = (modes, Q, cycles, 2, Z, width)
    scratch = [
        pltpu.VMEM((L,), F32),
        pltpu.VMEM((1, nlat), F32),
        pltpu.VMEM(conv_weight.shape, F32),
        pltpu.SMEM(lat_offsets.shape, jnp.int32),
        pltpu.SMEM(lon_offsets.shape, jnp.int32),
        pltpu.VMEM((1, C), F32),
        pltpu.VMEM((cycles, nlon, width), BF16),
        pltpu.VMEM(table.shape, BF16),
        pltpu.VMEM(inverse.shape, BF16),
        pltpu.VMEM(perm.shape, BF16),
        pltpu.VMEM(basis.shape, F32),
        pltpu.VMEM((Y, 2, C, width), BF16),
        pltpu.VMEM((2 * C, 2 * width), BF16),
        pltpu.VMEM(up_weight.shape, BF16),
        pltpu.VMEM(down_weight.shape, BF16),
        pltpu.VMEM((modes, L, nlat), BF16),
        pltpu.VMEM((modes, nlat, L), BF16),
        pltpu.VMEM(around_z, BF16),
        pltpu.VMEM(around_z, BF16),
        pltpu.VMEM(around_q, BF16),
        pltpu.VMEM(around_q, BF16),
        pltpu.VMEM((modes, Y, (cycles - 1) * Q * Z, 2 * width), BF16),
        pltpu.VMEM(around_back, BF16),
        pltpu.VMEM(around_back, BF16),
        pltpu.VMEM(around_z, BF16),
        pltpu.VMEM(around_z, BF16),
        pltpu.VMEM((2, nlon, width), BF16),
        pltpu.VMEM((cycles + 2, nlon + 2 * pad, width), F32),
        pltpu.VMEM((cycles - 1, nlon, width), F32),
        pltpu.VMEM((nlon, 2 * width), F32),
        pltpu.VMEM((nlon, width), BF16),
        pltpu.VMEM((Y, size, width), BF16),
        pltpu.VMEM((2, nlon, width), BF16),
        pltpu.VMEM((Y, 2, size, width), BF16),
        pltpu.VMEM((cycles - 1, nlon, width), BF16),
        pltpu.VMEM((cycles - 1, Y, size, width), BF16),
        pltpu.VMEM((cycles, Y, size, width), BF16),
        pltpu.SemaphoreType.DMA((13 + modes,)),
        pltpu.SemaphoreType.DMA((n_sem,)),
        pltpu.SemaphoreType.DMA((n_sem,)),
    ]
    return pl.pallas_call(
        functools.partial(block_kernel, dims),
        out_shape=pltpu.VMEM(grid.shape, BF16),
        in_specs=[any_space] * 14,
        out_specs=vmem,
        scratch_shapes=scratch,
        compiler_params=pltpu.CompilerParams(
            collective_id=0, has_side_effects=True, vmem_limit_bytes=56 * 1024 * 1024
        ),
        name="block",
    )(
        grid,
        jnp.asarray(table),
        jnp.asarray(inverse),
        jnp.asarray(perm),
        basis,
        mix_weight,
        spectral_gain,
        jnp.asarray(quad),
        conv_weight,
        lat_offsets,
        lon_offsets,
        ln_gain.reshape(1, C),
        up_weight,
        down_weight,
    )


def build(finer):
    sizes = tuple(finer.shape[a] for a in (*LAT, "chan"))
    return jax.shard_map(
        functools.partial(on_device, sizes),
        mesh=finer,
        in_specs=(
            P(LAT, None, "chan"),
            P(LAT, None, None),
            P(None, None, "chan"),
            P(),
            P(None, "chan"),
            P(),
            P(),
            P(),
            P(),
            P(),
        ),
        out_specs=P(LAT, None, "chan"),
        check_vma=False,
    )


def solution(mesh):
    return build(
        Mesh(mesh.devices.reshape(4, 16, 2, mesh.shape["chan"]), (*LAT, "chan"))
    )
```

```python
import functools
import math

import jax
import jax.numpy as jnp
import ml_dtypes
import numpy as np
from jax import lax
from jax.experimental import pallas as pl
from jax.experimental.pallas import tpu as pltpu
from jax.sharding import Mesh
from jax.sharding import PartitionSpec as P

LAT = ("lat_0", "lat_1", "lat_2")
MESH_ID = pl.DeviceIdType.MESH
TILE = 16
F32 = jnp.float32
BF16 = jnp.bfloat16


def transform_tables(X, Z, K, modes, nlon):
    j, z, ri, x, k = np.meshgrid(
        np.arange(modes), np.arange(Z), np.arange(2), np.arange(X), np.arange(K), indexing="ij"
    )
    m = (((x * Z + z) * K + k) * modes + j).reshape(modes, -1).astype(np.int64)
    part = ri.reshape(modes, -1)
    points = np.arange(nlon, dtype=np.int64)
    phase = (m[:, :, None] * points) % nlon
    angle = np.float32(2.0 * math.pi) * phase.astype(np.float32) / np.float32(nlon)
    table = np.where(part[:, :, None] == 0, np.cos(angle), -np.sin(angle)).astype(np.float32)
    return table.astype(ml_dtypes.bfloat16)


def cycle_order(X, Z, K, cycles):
    c, x, k, z = np.meshgrid(
        np.arange(cycles), np.arange(X), np.arange(K), np.arange(Z), indexing="ij"
    )
    return (((x * Z + z) * K + k) * cycles + c).reshape(-1)


def block_kernel(
    dims,
    grid_in,
    table_in,
    inverse_in,
    perm_in,
    basis_in,
    mix_in,
    gain_hbm,
    quad_hbm,
    conv_hbm,
    lat_hbm,
    lon_hbm,
    norm_hbm,
    up_in,
    down_in,
    out,
    gain_in,
    quad_in,
    conv_in,
    lat_off,
    lon_off,
    norm_in,
    grid_v,
    table,
    inverse,
    perm,
    basis,
    mix_all,
    mix_w,
    up_w,
    down_w,
    leg,
    leg_t,
    z1_send,
    z1_recv,
    x1_send,
    x1_recv,
    rows_send,
    gathered,
    mixed_send,
    x2_send,
    x2_recv,
    late_recv,
    z2_send,
    z2_recv,
    halo,
    padded,
    base,
    fields0,
    local_send,
    local_recv,
    field_send,
    field_recv,
    sum_send,
    sum_recv,
    out_send,
    load_sem,
    send_sem,
    recv_sem,
):
    X, Z, K, Y, cycles, modes, L, nlon, width, step, size = dims
    Q = X * K
    R = Q * Z
    x = lax.axis_index("lat_0")
    z = lax.axis_index("lat_1")
    k = lax.axis_index("lat_2")
    y = lax.axis_index("chan")
    q = x * K + k
    rank = (x * Z + z) * K + k
    last = modes - 1
    early = pl.ds(0, last)
    plane = Q * Z
    has_own = k == lax.rem(y, K)
    n_late = (cycles - 1) * Q
    pad = (padded.shape[1] - nlon) // 2

    loads = []
    middle = nlon // 2 // TILE * TILE
    for low, rows in ((0, middle), (middle, nlon - middle)):
        piece = pl.ds(low, rows)
        loads += [(grid_in.at[c, piece], grid_v.at[c, piece]) for c in range(cycles)]
    quarter = 2 * R // 4
    for i in range(4):
        piece = pl.ds(i * quarter, quarter)
        loads.append((table_in.at[0, piece], table.at[0, piece]))
    FIRST = len(loads)
    loads += [(table_in.at[j], table.at[j]) for j in range(1, modes)]
    BASIS = len(loads)
    loads += [(basis_in, basis), (perm_in, perm), (mix_in, mix_all.at[y])]
    loads += [(gain_hbm, gain_in), (quad_hbm, quad_in)]
    REST = len(loads)
    loads += [(inverse_in, inverse), (up_in, up_w), (down_in, down_w)]
    loads += [(conv_hbm, conv_in), (lat_hbm, lat_off), (lon_hbm, lon_off), (norm_hbm, norm_in)]
    copies = [
        pltpu.make_async_copy(src, dst, load_sem.at[i]) for i, (src, dst) in enumerate(loads)
    ]
    def q_device(other):
        return {"lat_0": other // K, "lat_2": lax.rem(other, K)}

    def rank_device(r):
        return {"lat_0": r // (Z * K), "lat_1": lax.rem(r // K, Z), "lat_2": lax.rem(r, K)}

    barrier = pltpu.get_barrier_semaphore()

    def greet(device):
        pl.semaphore_signal(barrier, inc=1, device_id=device, device_id_type=MESH_ID)

    def ring_place(i):
        far = Z - 1 - i
        offset = jnp.where(lax.rem(far, 2) == 1, (far + 1) // 2, Z - far // 2)
        return lax.rem(z + offset, Z)

    for copy in copies[:FIRST]:
        copy.start()

    @pl.loop(0, Z - 1)
    def _(i):
        greet({"lat_1": ring_place(i)})

    @pl.loop(1, Q * Y)
    def _(i):
        other = lax.rem(q * Y + y + i, Q * Y)
        greet({**q_device(other // Y), "chan": lax.rem(other, Y)})

    @pl.when(rank > 0)
    def _():
        greet(rank_device(rank - 1))

    @pl.when(rank < R - 1)
    def _():
        greet(rank_device(rank + 1))

    def send(src, dst, at, device):
        pltpu.make_async_remote_copy(
            src_ref=src,
            dst_ref=dst,
            send_sem=send_sem.at[at],
            recv_sem=recv_sem.at[at],
            device_id=device,
            device_id_type=MESH_ID,
        ).start()

    def await_recv(ref, at):
        pltpu.make_async_copy(ref, ref, recv_sem.at[at]).wait()

    def await_send(ref, at):
        pltpu.make_async_copy(ref, ref, send_sem.at[at]).wait()

    Z1, X1, X2, X2_REST, GATHER = (n * modes for n in range(5))
    EARLY = 5 * modes
    LAST = EARLY + cycles
    FIELD = LAST + cycles
    OUT = FIELD + cycles
    EXTRA = OUT + cycles
    LOCAL = EXTRA + cycles
    MIX = LOCAL + 1
    BEFORE = LOCAL + 2
    AFTER = LOCAL + 3
    FIELD_TAIL = LOCAL + 4
    OUT_TAIL = FIELD_TAIL + cycles
    cut = size // 2 // TILE * TILE

    def forward(j):
        points = jnp.concatenate([grid_v[c] for c in range(cycles)], axis=1)
        spec = jnp.dot(table[j], points, preferred_element_type=F32) * (1.0 / nlon)
        spec = spec.astype(BF16)
        for c in range(cycles):
            z1_send[j, :, c] = spec[:, c * width : (c + 1) * width].reshape(Z, 2 * Q, width)

    def send_z(buf, land, j, at):
        @pl.loop(0, Z - 1)
        def _(i):
            other = ring_place(i)
            send(buf.at[j, other], land.at[j, z], at + j, {"lat_1": other})

        land[j, z] = buf[j, z]

    def send_q(buf, land, j, at):
        @pl.loop(1, Q)
        def _(i):
            other = lax.rem(q + i, Q)
            send(buf.at[j, other], land.at[j, q], at + j, q_device(other))

        land[j, q] = buf[j, q]

    for copy in copies[:FIRST]:
        copy.wait()
    for copy in copies[FIRST:]:
        copy.start()
    forward(0)
    greeted = (Z - 1) + (Q * Y - 1)
    greeted = greeted + jnp.where(rank > 0, 1, 0) + jnp.where(rank < R - 1, 1, 0)
    pl.semaphore_wait(barrier, greeted)
    send_z(z1_send, z1_recv, 0, Z1)

    for j in range(1, modes):
        copies[FIRST - 1 + j].wait()
        forward(j)
        send_z(z1_send, z1_recv, j, Z1)

    @pl.when(rank < R - 1)
    def _():
        send(grid_v.at[cycles - 1], halo.at[0], BEFORE, rank_device(rank + 1))

    @pl.when(rank > 0)
    def _():
        send(grid_v.at[0], halo.at[1], AFTER, rank_device(rank - 1))

    copies[BASIS].wait()
    copies[BASIS + 1].wait()
    copies[BASIS + 2].wait()
    copies[BASIS + 3].wait()
    copies[BASIS + 4].wait()

    @pl.loop(1, Y)
    def _(i):
        send(mix_all.at[y], mix_all.at[y], MIX, {"chan": lax.rem(y + i, Y)})

    for j in range(modes):
        weighted = (basis[j] * quad_in[...]).astype(BF16)
        leg[j] = lax.dot_general(
            weighted, perm[...], (((1,), (1,)), ((), ())), preferred_element_type=F32
        ).astype(BF16)
        leg_t[j] = lax.dot_general(
            perm[...], basis[j].astype(BF16), (((1,), (1,)), ((), ())), preferred_element_type=F32
        ).astype(BF16)
    gain = jnp.transpose(jnp.broadcast_to(gain_in[...].reshape(1, L), (width, L)))

    def to_owners(j):
        await_recv(z1_recv.at[j, pl.ds(0, Z - 1)], Z1 + j)
        for c in range(cycles):
            turned = jnp.swapaxes(z1_recv[j, :, c].astype(F32), 0, 1).astype(BF16)
            for part in range(2):
                x1_send[j, :, part, c] = turned[part * Q : (part + 1) * Q]
        send_q(x1_send, x1_recv, j, X1)

    def build_weights():
        await_recv(mix_all.at[pl.ds(0, Y - 1)], MIX)
        for b in range(Y):
            left = slice(2 * b * width, (2 * b + 1) * width)
            right = slice((2 * b + 1) * width, (2 * b + 2) * width)
            for a in range(Y):
                real = mix_all[b, 0, a * width : (a + 1) * width, :]
                imag = mix_all[b, 1, a * width : (a + 1) * width, :]
                at = 2 * a * width
                mix_w[at : at + width, left] = real
                mix_w[at : at + width, right] = imag
                mix_w[at + width : at + 2 * width, left] = -imag
                mix_w[at + width : at + 2 * width, right] = real

    def legendre(j):
        await_recv(x1_recv.at[j, pl.ds(0, Q - 1)], X1 + j)
        parts = [
            jnp.concatenate(
                [x1_recv[j, :, part, c].reshape(plane, width) for c in range(cycles)], axis=0
            )
            for part in range(2)
        ]
        values = jnp.concatenate(parts, axis=1)
        found = jnp.dot(leg[j], values, preferred_element_type=F32)
        weight = jnp.where(rank * modes + j == 0, 1.0, 2.0).astype(F32)
        scale = gain * weight
        scaled = (found * jnp.concatenate([scale, scale], axis=1)).astype(BF16)
        back = jnp.dot(leg_t[j], scaled, preferred_element_type=F32).astype(BF16)
        for part in range(2):
            piece = back[:plane, part * width : (part + 1) * width]
            x2_send[j, :, part] = piece.reshape(Q, Z, width)

        @pl.loop(1, Q)
        def _(i):
            other = lax.rem(q + i, Q)
            send(x2_send.at[j, other], x2_recv.at[j, q], X2 + j, q_device(other))

        x2_recv[j, q] = x2_send[j, q]
        rows = back[plane:].reshape(cycles - 1, X, K, Z, 2 * width)
        for a in range(Y):
            rows_send[j, a] = rows[a // K, :, a % K]

        @pl.loop(1, Y)
        def _(i):
            other = lax.rem(y + i, Y)
            send(rows_send.at[j, other], gathered.at[j, y], GATHER + j, {"chan": other})

        gathered[j, y] = rows_send[j, y]

    def mix(j):
        await_recv(gathered.at[j, pl.ds(0, Y - 1)], GATHER + j)
        values = jnp.concatenate(
            [gathered[j, a].reshape(X * Z, 2 * width) for a in range(Y)], axis=1
        )
        mixed = jnp.dot(values, mix_w[...], preferred_element_type=F32).astype(BF16)
        for b in range(Y):
            for part in range(2):
                at = (2 * b + part) * width
                mixed_send[j, :, b, part] = mixed[:, at : at + width].reshape(X, Z, width)
        slot = (y // K) * Q + q

        @pl.loop(0, X * Y)
        def _(n):
            to_x = lax.rem(x + n // Y, X)
            other = lax.rem(y + n + 1, Y)

            @pl.when(jnp.logical_or(to_x * K + lax.rem(y, K) != q, other != y))
            def _():
                send(
                    mixed_send.at[j, to_x, other],
                    late_recv.at[j, slot],
                    X2_REST + j,
                    {"lat_0": to_x, "lat_2": lax.rem(y, K), "chan": other},
                )

        @pl.when(has_own)
        def _():
            late_recv[j, slot] = mixed_send[j, x, y]

    def all_but_own(wait, j):
        @pl.when(has_own)
        def _():
            wait(late_recv.at[j, pl.ds(0, n_late - 1)], X2_REST + j)

        @pl.when(jnp.logical_not(has_own))
        def _():
            wait(late_recv.at[j, pl.ds(0, n_late)], X2_REST + j)

    def to_cycles(j, which):
        if which == [0]:
            await_recv(x2_recv.at[j, pl.ds(0, Q - 1)], X2 + j)
        else:
            all_but_own(await_recv, j)
        for c in which:
            land, lead = (x2_recv, 0) if c == 0 else (late_recv, (c - 1) * Q)
            parts = [land[j, lead + a, part].astype(F32) for part in range(2) for a in range(Q)]
            z2_send[j, :, c] = jnp.swapaxes(jnp.stack(parts), 0, 1).astype(BF16)

            @pl.loop(0, Z - 1)
            def _(i):
                other = ring_place(i)
                send(
                    z2_send.at[j, other, c],
                    z2_recv.at[j, z, c],
                    (LAST if j == last else EARLY) + c,
                    {"lat_1": other},
                )

            z2_recv[j, z, c] = z2_send[j, z, c]

    def place(at, values):
        padded[at, pad : pad + nlon] = values
        padded[at, 0:pad] = values[nlon - pad :]
        padded[at, pad + nlon :] = values[:pad]

    def pad_field():
        for c in range(cycles):
            place(c + 1, grid_v[c].astype(F32))

        @pl.when(rank > 0)
        def _():
            await_recv(halo.at[0], BEFORE)
            place(0, halo[0].astype(F32))

        @pl.when(rank == 0)
        def _():
            padded[0] = jnp.zeros(padded.shape[1:], F32)

        @pl.when(rank < R - 1)
        def _():
            await_recv(halo.at[1], AFTER)
            place(cycles + 1, halo[1].astype(F32))

        @pl.when(rank == R - 1)
        def _():
            padded[cycles + 1] = jnp.zeros(padded.shape[1:], F32)

    def sine(cycle):
        angle = jnp.full((1, width), cycle, jnp.int32).astype(F32)
        return jnp.sin(math.pi * (angle + 0.5) / (R * cycles))

    def local_field(c):
        taps = conv_in.shape[0]
        block = 5 * TILE if nlon % (5 * TILE) == 0 else TILE
        own = rank * cycles + c
        here = sine(own)
        weights = [
            conv_in[tap : tap + 1, :] * (sine(own + lat_off[tap]) / here) for tap in range(taps)
        ]

        @pl.loop(0, nlon // block)
        def _(b):
            first = pl.multiple_of(b * block, TILE)
            total = padded[c + 1, pl.ds(pad + first, block), :]
            for tap in range(taps):
                source = padded[c + 1 + lat_off[tap], pl.ds(pad + first + lon_off[tap], block), :]
                total = total + weights[tap] * source
            if c == 0:
                local_send[pl.ds(first, block), :] = total.astype(BF16)
            else:
                base[c - 1, pl.ds(first, block), :] = total

    mine = pl.multiple_of(y * step, TILE)

    def share(src, dst, at, low=0, rows=None):
        rows = size if rows is None else rows

        @pl.loop(1, Y)
        def _(i):
            other = lax.rem(y + i, Y)
            first = pl.multiple_of(other * step, TILE) + low
            lead = (slice(None),) * (len(src.shape) - 2)
            send(
                src.at[(*lead, pl.ds(first, rows))],
                dst.at[(y, *lead, pl.ds(low, rows))],
                at,
                {"chan": other},
            )

    def share_local():
        pad_field()
        for c in range(cycles):
            local_field(c)
        share(local_send, local_recv, LOCAL)
        local_recv[y] = local_send[pl.ds(mine, size)]

    later = list(range(1, cycles))
    to_owners(0)
    legendre(0)
    build_weights()
    for j in range(1, modes):
        to_owners(j)
        to_cycles(j - 1, [0])
        if j > 1:
            to_cycles(j - 2, later)
        legendre(j)
        mix(j - 1)
    for copy in copies[REST:]:
        copy.wait()
    share_local()
    to_cycles(last, [0])
    if last > 0:
        to_cycles(last - 1, later)
    def both_parts(value):
        wide = value.astype(F32)
        turned = jnp.concatenate([-wide[:, Q:], wide[:, :Q]], axis=1).astype(BF16)
        return [value.reshape(2 * R, width), turned.reshape(2 * R, width)]

    def values_of(j, c):
        value = z2_recv[j, :, c]
        if c == 0:
            return jnp.concatenate(both_parts(value), axis=1)
        return value.reshape(2 * R, width)

    def partly(c):
        await_recv(z2_recv.at[early, pl.ds(0, Z - 1), c], EARLY + c)
        found = base[c - 1] if c > 0 else None
        for j in range(last):
            term = jnp.dot(inverse[j], values_of(j, c), preferred_element_type=F32)
            found = term if found is None else found + term
        if c == 0:
            fields0[...] = found
        else:
            base[c - 1] = found

    def to_points(c):
        await_recv(z2_recv.at[last, pl.ds(0, Z - 1), c], LAST + c)
        found = fields0[...] if c == 0 else base[c - 1]
        found = found + jnp.dot(inverse[last], values_of(last, c), preferred_element_type=F32)
        if c == 0:
            fields = found.astype(BF16)
            field_send[0] = fields[:, :width]
            field_send[1] = fields[:, width:]
            share(field_send, field_recv, FIELD)
            field_recv[y] = field_send[:, pl.ds(mine, size)]
        else:
            sum_send[c - 1] = found.astype(BF16)
            share(sum_send.at[c - 1], sum_recv.at[c - 1], FIELD + c, 0, cut)
            share(sum_send.at[c - 1], sum_recv.at[c - 1], FIELD_TAIL + c, cut, size - cut)
            sum_recv[c - 1, y] = sum_send[c - 1, pl.ds(mine, size)]

    def perceptron(c, low=0, rows=None):
        rows = size if rows is None else rows
        own = slice(low, low + rows)
        out_at, field_at = (OUT + c, FIELD + c) if low == 0 else (OUT_TAIL + c, FIELD_TAIL + c)
        if c == 0:
            await_recv(field_recv.at[pl.ds(0, Y - 1)], FIELD)
            points = jnp.concatenate(
                [field_recv[a, part] for part in range(2) for a in range(Y)], axis=1
            )
            pieces = []
            for a in range(Y):
                weights = jnp.concatenate([mix_all[a, 0], mix_all[a, 1]], axis=0)
                pieces.append(jnp.dot(points, weights, preferred_element_type=F32))
            near = jnp.concatenate([local_recv[a] for a in range(Y)], axis=1)
            row = (jnp.concatenate(pieces, axis=1) + near.astype(F32)).astype(BF16)
        else:
            await_recv(sum_recv.at[c - 1, pl.ds(0, Y - 1), pl.ds(low, rows)], field_at)
            row = jnp.concatenate([sum_recv[c - 1, a, own] for a in range(Y)], axis=1)
        row = row.astype(F32)
        center = jnp.mean(row, axis=-1, keepdims=True)
        off = row - center
        spread = jnp.mean(off * off, axis=-1, keepdims=True)
        normed = (off / jnp.sqrt(spread + 1e-05) * norm_in[...]).astype(BF16)
        hidden = jax.nn.gelu(
            jnp.dot(normed, up_w[...], preferred_element_type=F32), approximate=True
        ).astype(BF16)
        result = (jnp.dot(hidden, down_w[...], preferred_element_type=F32) + row).astype(BF16)
        for a in range(Y):
            out_send[c, a, own] = result[:, a * width : (a + 1) * width]
        main = min(low + rows, step) - low
        extra = low + rows > step

        @pl.loop(1, Y)
        def _(i):
            other = lax.rem(y + i, Y)
            send(
                out_send.at[c, other, pl.ds(low, main)],
                out.at[c, pl.ds(mine + low, main)],
                out_at,
                {"chan": other},
            )

            if extra:

                @pl.when(y == Y - 1)
                def _():
                    send(
                        out_send.at[c, other, pl.ds(step, size - step)],
                        out.at[c, pl.ds(Y * step, size - step)],
                        EXTRA + c,
                        {"chan": other},
                    )

        out[c, pl.ds(mine + low, main), :] = out_send[c, y, low : low + main]

        if extra:

            @pl.when(y == Y - 1)
            def _():
                out[c, Y * step :, :] = out_send[c, y, step:]

    def out_pieces(c):
        if c == 0:
            return [(OUT + c, step)]
        return [(OUT + c, cut), (OUT_TAIL + c, step - cut)]

    def finish(c):
        for at, main in out_pieces(c):
            await_recv(out.at[c, pl.ds(0, (Y - 1) * main)], at)

        @pl.when(y < Y - 1)
        def _():
            await_recv(out.at[c, pl.ds(0, size - step)], EXTRA + c)


    partly(0)
    mix(last)
    to_points(0)
    to_cycles(last, later)
    partly(1)
    await_recv(local_recv.at[pl.ds(0, Y - 1)], LOCAL)
    perceptron(0)
    for c in range(1, cycles):
        if c > 1:
            partly(c)
        to_points(c)
    for c in range(1, cycles):
        perceptron(c, 0, cut)
        perceptron(c, cut, size - cut)
    for c in range(cycles):
        finish(c)

    for j in range(modes):
        await_send(z1_send.at[j, pl.ds(0, Z - 1)], Z1 + j)
        await_send(x1_send.at[j, pl.ds(0, Q - 1)], X1 + j)
        await_send(x2_send.at[j, pl.ds(0, Q - 1)], X2 + j)
        all_but_own(await_send, j)
        await_send(gathered.at[j, pl.ds(0, Y - 1)], GATHER + j)
    await_send(local_recv.at[pl.ds(0, Y - 1)], LOCAL)
    await_send(mix_all.at[pl.ds(0, Y - 1)], MIX)
    for c in range(cycles):
        await_send(z2_send.at[early, pl.ds(0, Z - 1), c], EARLY + c)
        await_send(z2_send.at[last, pl.ds(0, Z - 1), c], LAST + c)
        if c == 0:
            await_send(field_recv.at[pl.ds(0, Y - 1)], FIELD)
        else:
            await_send(sum_recv.at[c - 1, pl.ds(0, Y - 1), pl.ds(0, cut)], FIELD + c)
            await_send(sum_recv.at[c - 1, pl.ds(0, Y - 1), pl.ds(cut, size - cut)], FIELD_TAIL + c)
        for at, main in out_pieces(c):
            await_send(out.at[c, pl.ds(0, (Y - 1) * main)], at)

        @pl.when(y == Y - 1)
        def _():
            await_send(out.at[c, pl.ds(0, (Y - 1) * (size - step))], EXTRA + c)

    @pl.when(rank < R - 1)
    def _():
        await_send(halo.at[0], BEFORE)

    @pl.when(rank > 0)
    def _():
        await_send(halo.at[1], AFTER)


def on_device(
    sizes,
    grid,
    basis,
    mix_weight,
    spectral_gain,
    conv_weight,
    lat_offsets,
    lon_offsets,
    ln_gain,
    up_weight,
    down_weight,
):
    X, Z, K, Y = sizes
    cycles, nlon, width = grid.shape
    modes, L, nlat = basis.shape
    C = width * Y
    Q = X * K
    step = nlon // (Y * TILE) * TILE
    size = nlon - (Y - 1) * step
    table = transform_tables(X, Z, K, modes, nlon)
    inverse = np.ascontiguousarray(table.transpose(0, 2, 1))
    perm = np.zeros((nlat, nlat), ml_dtypes.bfloat16)
    perm[np.arange(nlat), cycle_order(X, Z, K, cycles)] = 1
    theta = (math.pi * (np.arange(nlat, dtype=np.float32) + np.float32(0.5)) / nlat).astype(
        np.float32
    )
    quad = (np.float32(math.pi / nlat) * np.sin(theta)).astype(np.float32)[None, :]
    dims = (X, Z, K, Y, cycles, modes, L, nlon, width, step, size)
    any_space = pl.BlockSpec(memory_space=pl.ANY)
    vmem = pl.BlockSpec(memory_space=pltpu.VMEM)
    pad = 8
    n_sem = 5 * modes + 7 * cycles + 4
    around_z = (modes, Z, cycles, 2 * Q, width)
    around_q = (modes, Q, 2, cycles, Z, width)
    scratch = [
        pltpu.VMEM((L,), F32),
        pltpu.VMEM((1, nlat), F32),
        pltpu.VMEM(conv_weight.shape, F32),
        pltpu.SMEM(lat_offsets.shape, jnp.int32),
        pltpu.SMEM(lon_offsets.shape, jnp.int32),
        pltpu.VMEM((1, C), F32),
        pltpu.VMEM((cycles, nlon, width), BF16),
        pltpu.VMEM(table.shape, BF16),
        pltpu.VMEM(inverse.shape, BF16),
        pltpu.VMEM(perm.shape, BF16),
        pltpu.VMEM(basis.shape, F32),
        pltpu.VMEM((Y, 2, C, width), BF16),
        pltpu.VMEM((2 * C, 2 * C), BF16),
        pltpu.VMEM(up_weight.shape, BF16),
        pltpu.VMEM(down_weight.shape, BF16),
        pltpu.VMEM((modes, L, nlat), BF16),
        pltpu.VMEM((modes, nlat, L), BF16),
        pltpu.VMEM(around_z, BF16),
        pltpu.VMEM(around_z, BF16),
        pltpu.VMEM(around_q, BF16),
        pltpu.VMEM(around_q, BF16),
        pltpu.VMEM((modes, Y, X, Z, 2 * width), BF16),
        pltpu.VMEM((modes, Y, X, Z, 2 * width), BF16),
        pltpu.VMEM((modes, X, Y, 2, Z, width), BF16),
        pltpu.VMEM((modes, Q, 2, Z, width), BF16),
        pltpu.VMEM((modes, Q, 2, Z, width), BF16),
        pltpu.VMEM((modes, (cycles - 1) * Q, 2, Z, width), BF16),
        pltpu.VMEM(around_z, BF16),
        pltpu.VMEM(around_z, BF16),
        pltpu.VMEM((2, nlon, width), BF16),
        pltpu.VMEM((cycles + 2, nlon + 2 * pad, width), F32),
        pltpu.VMEM((cycles - 1, nlon, width), F32),
        pltpu.VMEM((nlon, 2 * width), F32),
        pltpu.VMEM((nlon, width), BF16),
        pltpu.VMEM((Y, size, width), BF16),
        pltpu.VMEM((2, nlon, width), BF16),
        pltpu.VMEM((Y, 2, size, width), BF16),
        pltpu.VMEM((cycles - 1, nlon, width), BF16),
        pltpu.VMEM((cycles - 1, Y, size, width), BF16),
        pltpu.VMEM((cycles, Y, size, width), BF16),
        pltpu.SemaphoreType.DMA((2 * cycles + modes + 15,)),
        pltpu.SemaphoreType.DMA((n_sem,)),
        pltpu.SemaphoreType.DMA((n_sem,)),
    ]
    return pl.pallas_call(
        functools.partial(block_kernel, dims),
        out_shape=pltpu.VMEM(grid.shape, BF16),
        in_specs=[any_space] * 14,
        out_specs=vmem,
        scratch_shapes=scratch,
        compiler_params=pltpu.CompilerParams(
            collective_id=0, has_side_effects=True, vmem_limit_bytes=56 * 1024 * 1024
        ),
        name="block",
    )(
        grid,
        jnp.asarray(table),
        jnp.asarray(inverse),
        jnp.asarray(perm),
        basis,
        mix_weight,
        spectral_gain,
        jnp.asarray(quad),
        conv_weight,
        lat_offsets,
        lon_offsets,
        ln_gain.reshape(1, C),
        up_weight,
        down_weight,
    )


def build(finer):
    sizes = tuple(finer.shape[a] for a in (*LAT, "chan"))
    return jax.shard_map(
        functools.partial(on_device, sizes),
        mesh=finer,
        in_specs=(
            P(LAT, None, "chan"),
            P(LAT, None, None),
            P(None, None, "chan"),
            P(),
            P(None, "chan"),
            P(),
            P(),
            P(),
            P(),
            P(),
        ),
        out_specs=P(LAT, None, "chan"),
        check_vma=False,
    )


def solution(mesh):
    return build(
        Mesh(mesh.devices.reshape(4, 16, 2, mesh.shape["chan"]), (*LAT, "chan"))
    )
```

```python
import functools
import math

import jax
import jax.numpy as jnp
import ml_dtypes
import numpy as np
from jax import lax
from jax.experimental import pallas as pl
from jax.experimental.pallas import tpu as pltpu
from jax.sharding import Mesh
from jax.sharding import PartitionSpec as P

LAT = ("lat_0", "lat_1", "lat_2")
MESH_ID = pl.DeviceIdType.MESH
TILE = 16
F32 = jnp.float32
BF16 = jnp.bfloat16


def transform_tables(X, Z, K, modes, nlon):
    j, z, ri, x, k = np.meshgrid(
        np.arange(modes), np.arange(Z), np.arange(2), np.arange(X), np.arange(K), indexing="ij"
    )
    m = (((x * Z + z) * K + k) * modes + j).reshape(modes, -1).astype(np.int64)
    part = ri.reshape(modes, -1)
    points = np.arange(nlon, dtype=np.int64)
    phase = (m[:, :, None] * points) % nlon
    angle = np.float32(2.0 * math.pi) * phase.astype(np.float32) / np.float32(nlon)
    table = np.where(part[:, :, None] == 0, np.cos(angle), -np.sin(angle)).astype(np.float32)
    return table.astype(ml_dtypes.bfloat16)


def cycle_order(X, Z, K, cycles):
    c, x, k, z = np.meshgrid(
        np.arange(cycles), np.arange(X), np.arange(K), np.arange(Z), indexing="ij"
    )
    return (((x * Z + z) * K + k) * cycles + c).reshape(-1)


def block_kernel(
    dims,
    grid_in,
    table_in,
    inverse_in,
    perm_in,
    basis_in,
    mix_in,
    gain_hbm,
    quad_hbm,
    conv_hbm,
    lat_hbm,
    lon_hbm,
    norm_hbm,
    up_in,
    down_in,
    out,
    gain_in,
    quad_in,
    conv_in,
    lat_off,
    lon_off,
    norm_in,
    grid_v,
    table,
    inverse,
    perm,
    basis,
    mix_all,
    mix_w,
    up_w,
    down_w,
    leg,
    leg_t,
    z1_send,
    z1_recv,
    x1_send,
    x1_recv,
    rows_send,
    gathered,
    mixed_send,
    x2_send,
    x2_recv,
    late_recv,
    z2_send,
    z2_recv,
    halo,
    padded,
    base,
    fields0,
    local_send,
    local_recv,
    field_send,
    field_recv,
    sum_send,
    sum_recv,
    out_send,
    load_sem,
    send_sem,
    recv_sem,
):
    X, Z, K, Y, cycles, modes, L, nlon, width, step, size = dims
    Q = X * K
    R = Q * Z
    x = lax.axis_index("lat_0")
    z = lax.axis_index("lat_1")
    k = lax.axis_index("lat_2")
    y = lax.axis_index("chan")
    q = x * K + k
    rank = (x * Z + z) * K + k
    last = modes - 1
    early = pl.ds(0, last)
    plane = Q * Z
    has_own = k == lax.rem(y, K)
    n_late = (cycles - 1) * Q
    pad = (padded.shape[1] - nlon) // 2

    loads = []
    middle = nlon // 2 // TILE * TILE
    for low, rows in ((0, middle), (middle, nlon - middle)):
        piece = pl.ds(low, rows)
        loads += [(grid_in.at[c, piece], grid_v.at[c, piece]) for c in range(cycles)]
    quarter = 2 * R // 4
    for i in range(4):
        piece = pl.ds(i * quarter, quarter)
        loads.append((table_in.at[0, piece], table.at[0, piece]))
    FIRST = len(loads)
    loads += [(table_in.at[j], table.at[j]) for j in range(1, modes)]
    BASIS = len(loads)
    loads += [(basis_in, basis), (perm_in, perm), (mix_in, mix_all.at[y])]
    loads += [(gain_hbm, gain_in), (quad_hbm, quad_in)]
    REST = len(loads)
    loads += [(inverse_in, inverse), (up_in, up_w), (down_in, down_w)]
    loads += [(conv_hbm, conv_in), (lat_hbm, lat_off), (lon_hbm, lon_off), (norm_hbm, norm_in)]
    copies = [
        pltpu.make_async_copy(src, dst, load_sem.at[i]) for i, (src, dst) in enumerate(loads)
    ]
    def q_device(other):
        return {"lat_0": other // K, "lat_2": lax.rem(other, K)}

    def rank_device(r):
        return {"lat_0": r // (Z * K), "lat_1": lax.rem(r // K, Z), "lat_2": lax.rem(r, K)}

    barrier = pltpu.get_barrier_semaphore()

    def greet(device):
        pl.semaphore_signal(barrier, inc=1, device_id=device, device_id_type=MESH_ID)

    def far_first(own, i, length):
        far = length - 1 - i
        offset = jnp.where(lax.rem(far, 2) == 1, (far + 1) // 2, length - far // 2)
        return lax.rem(own + offset, length)

    def ring_place(i):
        return far_first(z, i, Z)

    def q_place(i):
        return far_first(x, i // K, X) * K + lax.rem(k + 1 + lax.rem(i, K), K)

    for copy in copies[:FIRST]:
        copy.start()

    @pl.loop(0, Z - 1)
    def _(i):
        greet({"lat_1": ring_place(i)})

    @pl.loop(1, Q * Y)
    def _(i):
        other = lax.rem(q * Y + y + i, Q * Y)
        greet({**q_device(other // Y), "chan": lax.rem(other, Y)})

    @pl.when(rank > 0)
    def _():
        greet(rank_device(rank - 1))

    @pl.when(rank < R - 1)
    def _():
        greet(rank_device(rank + 1))

    def send(src, dst, at, device):
        pltpu.make_async_remote_copy(
            src_ref=src,
            dst_ref=dst,
            send_sem=send_sem.at[at],
            recv_sem=recv_sem.at[at],
            device_id=device,
            device_id_type=MESH_ID,
        ).start()

    def await_recv(ref, at):
        pltpu.make_async_copy(ref, ref, recv_sem.at[at]).wait()

    def await_send(ref, at):
        pltpu.make_async_copy(ref, ref, send_sem.at[at]).wait()

    Z1, X1, X2, X2_REST, GATHER = (n * modes for n in range(5))
    EARLY = 5 * modes
    LAST = EARLY + cycles
    FIELD = LAST + cycles
    OUT = FIELD + cycles
    EXTRA = OUT + cycles
    LOCAL = EXTRA + cycles
    MIX = LOCAL + 1
    BEFORE = LOCAL + 2
    AFTER = LOCAL + 3
    FIELD_TAIL = LOCAL + 4
    OUT_TAIL = FIELD_TAIL + cycles
    cut = size // 2 // TILE * TILE

    def forward(j):
        points = jnp.concatenate([grid_v[c] for c in range(cycles)], axis=1)
        spec = jnp.dot(table[j], points, preferred_element_type=F32) * (1.0 / nlon)
        spec = spec.astype(BF16)
        for c in range(cycles):
            z1_send[j, :, c] = spec[:, c * width : (c + 1) * width].reshape(Z, 2 * Q, width)

    def send_z(buf, land, j, at):
        @pl.loop(0, Z - 1)
        def _(i):
            other = ring_place(i)
            send(buf.at[j, other], land.at[j, z], at + j, {"lat_1": other})

        land[j, z] = buf[j, z]

    def send_q(buf, land, j, at):
        @pl.loop(0, Q - 1)
        def _(i):
            other = q_place(i)
            send(buf.at[j, other], land.at[j, q], at + j, q_device(other))

        land[j, q] = buf[j, q]

    for copy in copies[:FIRST]:
        copy.wait()
    for copy in copies[FIRST:]:
        copy.start()
    forward(0)
    greeted = (Z - 1) + (Q * Y - 1)
    greeted = greeted + jnp.where(rank > 0, 1, 0) + jnp.where(rank < R - 1, 1, 0)
    pl.semaphore_wait(barrier, greeted)
    send_z(z1_send, z1_recv, 0, Z1)

    for j in range(1, modes):
        copies[FIRST - 1 + j].wait()
        forward(j)
        send_z(z1_send, z1_recv, j, Z1)

    @pl.when(rank < R - 1)
    def _():
        send(grid_v.at[cycles - 1], halo.at[0], BEFORE, rank_device(rank + 1))

    @pl.when(rank > 0)
    def _():
        send(grid_v.at[0], halo.at[1], AFTER, rank_device(rank - 1))

    copies[BASIS].wait()
    copies[BASIS + 1].wait()
    copies[BASIS + 2].wait()
    copies[BASIS + 3].wait()
    copies[BASIS + 4].wait()

    @pl.loop(1, Y)
    def _(i):
        send(mix_all.at[y], mix_all.at[y], MIX, {"chan": lax.rem(y + i, Y)})

    for j in range(modes):
        weighted = (basis[j] * quad_in[...]).astype(BF16)
        leg[j] = lax.dot_general(
            weighted, perm[...], (((1,), (1,)), ((), ())), preferred_element_type=F32
        ).astype(BF16)
        leg_t[j] = lax.dot_general(
            perm[...], basis[j].astype(BF16), (((1,), (1,)), ((), ())), preferred_element_type=F32
        ).astype(BF16)
    gain = jnp.transpose(jnp.broadcast_to(gain_in[...].reshape(1, L), (width, L)))

    def to_owners(j):
        await_recv(z1_recv.at[j, pl.ds(0, Z - 1)], Z1 + j)
        for c in range(cycles):
            turned = jnp.swapaxes(z1_recv[j, :, c].astype(F32), 0, 1).astype(BF16)
            for part in range(2):
                x1_send[j, :, part, c] = turned[part * Q : (part + 1) * Q]
        send_q(x1_send, x1_recv, j, X1)

    def build_weights():
        await_recv(mix_all.at[pl.ds(0, Y - 1)], MIX)
        for b in range(Y):
            left = slice(2 * b * width, (2 * b + 1) * width)
            right = slice((2 * b + 1) * width, (2 * b + 2) * width)
            for a in range(Y):
                real = mix_all[b, 0, a * width : (a + 1) * width, :]
                imag = mix_all[b, 1, a * width : (a + 1) * width, :]
                at = 2 * a * width
                mix_w[at : at + width, left] = real
                mix_w[at : at + width, right] = imag
                mix_w[at + width : at + 2 * width, left] = -imag
                mix_w[at + width : at + 2 * width, right] = real

    def legendre(j):
        await_recv(x1_recv.at[j, pl.ds(0, Q - 1)], X1 + j)
        parts = [
            jnp.concatenate(
                [x1_recv[j, :, part, c].reshape(plane, width) for c in range(cycles)], axis=0
            )
            for part in range(2)
        ]
        values = jnp.concatenate(parts, axis=1)
        found = jnp.dot(leg[j], values, preferred_element_type=F32)
        weight = jnp.where(rank * modes + j == 0, 1.0, 2.0).astype(F32)
        scale = gain * weight
        scaled = (found * jnp.concatenate([scale, scale], axis=1)).astype(BF16)
        back = jnp.dot(leg_t[j], scaled, preferred_element_type=F32).astype(BF16)
        for part in range(2):
            piece = back[:plane, part * width : (part + 1) * width]
            x2_send[j, :, part] = piece.reshape(Q, Z, width)

        @pl.loop(0, Q - 1)
        def _(i):
            other = q_place(i)
            send(x2_send.at[j, other], x2_recv.at[j, q], X2 + j, q_device(other))

        x2_recv[j, q] = x2_send[j, q]
        rows = back[plane:].reshape(cycles - 1, X, K, Z, 2 * width)
        for a in range(Y):
            rows_send[j, a] = rows[a // K, :, a % K]

        @pl.loop(0, Y - 1)
        def _(i):
            other = far_first(y, i, Y)
            send(rows_send.at[j, other], gathered.at[j, y], GATHER + j, {"chan": other})

        gathered[j, y] = rows_send[j, y]

    def mix(j):
        await_recv(gathered.at[j, pl.ds(0, Y - 1)], GATHER + j)
        values = jnp.concatenate(
            [gathered[j, a].reshape(X * Z, 2 * width) for a in range(Y)], axis=1
        )
        mixed = jnp.dot(values, mix_w[...], preferred_element_type=F32).astype(BF16)
        for b in range(Y):
            for part in range(2):
                at = (2 * b + part) * width
                mixed_send[j, :, b, part] = mixed[:, at : at + width].reshape(X, Z, width)
        slot = (y // K) * Q + q

        @pl.loop(0, X * Y)
        def _(n):
            to_x = far_first(x, n // Y, X)
            other = far_first(y, lax.rem(n, Y), Y)

            @pl.when(jnp.logical_or(to_x * K + lax.rem(y, K) != q, other != y))
            def _():
                send(
                    mixed_send.at[j, to_x, other],
                    late_recv.at[j, slot],
                    X2_REST + j,
                    {"lat_0": to_x, "lat_2": lax.rem(y, K), "chan": other},
                )

        @pl.when(has_own)
        def _():
            late_recv[j, slot] = mixed_send[j, x, y]

    def all_but_own(wait, j):
        @pl.when(has_own)
        def _():
            wait(late_recv.at[j, pl.ds(0, n_late - 1)], X2_REST + j)

        @pl.when(jnp.logical_not(has_own))
        def _():
            wait(late_recv.at[j, pl.ds(0, n_late)], X2_REST + j)

    def to_cycles(j, which):
        if which == [0]:
            await_recv(x2_recv.at[j, pl.ds(0, Q - 1)], X2 + j)
        else:
            all_but_own(await_recv, j)
        for c in which:
            land, lead = (x2_recv, 0) if c == 0 else (late_recv, (c - 1) * Q)
            parts = [land[j, lead + a, part].astype(F32) for part in range(2) for a in range(Q)]
            z2_send[j, :, c] = jnp.swapaxes(jnp.stack(parts), 0, 1).astype(BF16)

            @pl.loop(0, Z - 1)
            def _(i):
                other = ring_place(i)
                send(
                    z2_send.at[j, other, c],
                    z2_recv.at[j, z, c],
                    (LAST if j == last else EARLY) + c,
                    {"lat_1": other},
                )

            z2_recv[j, z, c] = z2_send[j, z, c]

    def place(at, values):
        padded[at, pad : pad + nlon] = values
        padded[at, 0:pad] = values[nlon - pad :]
        padded[at, pad + nlon :] = values[:pad]

    def pad_field():
        for c in range(cycles):
            place(c + 1, grid_v[c].astype(F32))

        @pl.when(rank > 0)
        def _():
            await_recv(halo.at[0], BEFORE)
            place(0, halo[0].astype(F32))

        @pl.when(rank == 0)
        def _():
            padded[0] = jnp.zeros(padded.shape[1:], F32)

        @pl.when(rank < R - 1)
        def _():
            await_recv(halo.at[1], AFTER)
            place(cycles + 1, halo[1].astype(F32))

        @pl.when(rank == R - 1)
        def _():
            padded[cycles + 1] = jnp.zeros(padded.shape[1:], F32)

    def sine(cycle):
        angle = jnp.full((1, width), cycle, jnp.int32).astype(F32)
        return jnp.sin(math.pi * (angle + 0.5) / (R * cycles))

    def local_field(c):
        taps = conv_in.shape[0]
        block = 5 * TILE if nlon % (5 * TILE) == 0 else TILE
        own = rank * cycles + c
        here = sine(own)
        weights = [
            conv_in[tap : tap + 1, :] * (sine(own + lat_off[tap]) / here) for tap in range(taps)
        ]

        @pl.loop(0, nlon // block)
        def _(b):
            first = pl.multiple_of(b * block, TILE)
            total = padded[c + 1, pl.ds(pad + first, block), :]
            for tap in range(taps):
                source = padded[c + 1 + lat_off[tap], pl.ds(pad + first + lon_off[tap], block), :]
                total = total + weights[tap] * source
            if c == 0:
                local_send[pl.ds(first, block), :] = total.astype(BF16)
            else:
                base[c - 1, pl.ds(first, block), :] = total

    mine = pl.multiple_of(y * step, TILE)

    def share(src, dst, at, low=0, rows=None):
        rows = size if rows is None else rows

        @pl.loop(0, Y - 1)
        def _(i):
            other = far_first(y, i, Y)
            first = pl.multiple_of(other * step, TILE) + low
            lead = (slice(None),) * (len(src.shape) - 2)
            send(
                src.at[(*lead, pl.ds(first, rows))],
                dst.at[(y, *lead, pl.ds(low, rows))],
                at,
                {"chan": other},
            )

    def share_local():
        pad_field()
        for c in range(cycles):
            local_field(c)
        share(local_send, local_recv, LOCAL)
        local_recv[y] = local_send[pl.ds(mine, size)]

    later = list(range(1, cycles))
    to_owners(0)
    legendre(0)
    build_weights()
    for j in range(1, modes):
        to_owners(j)
        to_cycles(j - 1, [0])
        if j > 1:
            to_cycles(j - 2, later)
        legendre(j)
        mix(j - 1)
    for copy in copies[REST:]:
        copy.wait()
    share_local()
    to_cycles(last, [0])
    if last > 0:
        to_cycles(last - 1, later)
    def both_parts(value):
        wide = value.astype(F32)
        turned = jnp.concatenate([-wide[:, Q:], wide[:, :Q]], axis=1).astype(BF16)
        return [value.reshape(2 * R, width), turned.reshape(2 * R, width)]

    def values_of(j, c):
        value = z2_recv[j, :, c]
        if c == 0:
            return jnp.concatenate(both_parts(value), axis=1)
        return value.reshape(2 * R, width)

    def partly(c):
        await_recv(z2_recv.at[early, pl.ds(0, Z - 1), c], EARLY + c)
        found = base[c - 1] if c > 0 else None
        for j in range(last):
            term = jnp.dot(inverse[j], values_of(j, c), preferred_element_type=F32)
            found = term if found is None else found + term
        if c == 0:
            fields0[...] = found
        else:
            base[c - 1] = found

    def to_points(c):
        await_recv(z2_recv.at[last, pl.ds(0, Z - 1), c], LAST + c)
        found = fields0[...] if c == 0 else base[c - 1]
        found = found + jnp.dot(inverse[last], values_of(last, c), preferred_element_type=F32)
        if c == 0:
            fields = found.astype(BF16)
            field_send[0] = fields[:, :width]
            field_send[1] = fields[:, width:]
            share(field_send, field_recv, FIELD)
            field_recv[y] = field_send[:, pl.ds(mine, size)]
        else:
            sum_send[c - 1] = found.astype(BF16)
            share(sum_send.at[c - 1], sum_recv.at[c - 1], FIELD + c, 0, cut)
            share(sum_send.at[c - 1], sum_recv.at[c - 1], FIELD_TAIL + c, cut, size - cut)
            sum_recv[c - 1, y] = sum_send[c - 1, pl.ds(mine, size)]

    def perceptron(c, low=0, rows=None):
        rows = size if rows is None else rows
        own = slice(low, low + rows)
        out_at, field_at = (OUT + c, FIELD + c) if low == 0 else (OUT_TAIL + c, FIELD_TAIL + c)
        if c == 0:
            await_recv(field_recv.at[pl.ds(0, Y - 1)], FIELD)
            points = jnp.concatenate(
                [field_recv[a, part] for part in range(2) for a in range(Y)], axis=1
            )
            pieces = []
            for a in range(Y):
                weights = jnp.concatenate([mix_all[a, 0], mix_all[a, 1]], axis=0)
                pieces.append(jnp.dot(points, weights, preferred_element_type=F32))
            near = jnp.concatenate([local_recv[a] for a in range(Y)], axis=1)
            row = (jnp.concatenate(pieces, axis=1) + near.astype(F32)).astype(BF16)
        else:
            await_recv(sum_recv.at[c - 1, pl.ds(0, Y - 1), pl.ds(low, rows)], field_at)
            row = jnp.concatenate([sum_recv[c - 1, a, own] for a in range(Y)], axis=1)
        row = row.astype(F32)
        center = jnp.mean(row, axis=-1, keepdims=True)
        off = row - center
        spread = jnp.mean(off * off, axis=-1, keepdims=True)
        normed = (off / jnp.sqrt(spread + 1e-05) * norm_in[...]).astype(BF16)
        hidden = jax.nn.gelu(
            jnp.dot(normed, up_w[...], preferred_element_type=F32), approximate=True
        ).astype(BF16)
        result = (jnp.dot(hidden, down_w[...], preferred_element_type=F32) + row).astype(BF16)
        for a in range(Y):
            out_send[c, a, own] = result[:, a * width : (a + 1) * width]
        main = min(low + rows, step) - low
        extra = low + rows > step

        @pl.loop(0, Y - 1)
        def _(i):
            other = far_first(y, i, Y)
            send(
                out_send.at[c, other, pl.ds(low, main)],
                out.at[c, pl.ds(mine + low, main)],
                out_at,
                {"chan": other},
            )

            if extra:

                @pl.when(y == Y - 1)
                def _():
                    send(
                        out_send.at[c, other, pl.ds(step, size - step)],
                        out.at[c, pl.ds(Y * step, size - step)],
                        EXTRA + c,
                        {"chan": other},
                    )

        out[c, pl.ds(mine + low, main), :] = out_send[c, y, low : low + main]

        if extra:

            @pl.when(y == Y - 1)
            def _():
                out[c, Y * step :, :] = out_send[c, y, step:]

    def out_pieces(c):
        if c == 0:
            return [(OUT + c, step)]
        return [(OUT + c, cut), (OUT_TAIL + c, step - cut)]

    def finish(c):
        for at, main in out_pieces(c):
            await_recv(out.at[c, pl.ds(0, (Y - 1) * main)], at)

        @pl.when(y < Y - 1)
        def _():
            await_recv(out.at[c, pl.ds(0, size - step)], EXTRA + c)


    partly(0)
    mix(last)
    to_points(0)
    to_cycles(last, later)
    partly(1)
    await_recv(local_recv.at[pl.ds(0, Y - 1)], LOCAL)
    perceptron(0)
    for c in range(1, cycles):
        if c > 1:
            partly(c)
        to_points(c)
    for c in range(1, cycles):
        perceptron(c, 0, cut)
        perceptron(c, cut, size - cut)
    for c in range(cycles):
        finish(c)

    for j in range(modes):
        await_send(z1_send.at[j, pl.ds(0, Z - 1)], Z1 + j)
        await_send(x1_send.at[j, pl.ds(0, Q - 1)], X1 + j)
        await_send(x2_send.at[j, pl.ds(0, Q - 1)], X2 + j)
        all_but_own(await_send, j)
        await_send(gathered.at[j, pl.ds(0, Y - 1)], GATHER + j)
    await_send(local_recv.at[pl.ds(0, Y - 1)], LOCAL)
    await_send(mix_all.at[pl.ds(0, Y - 1)], MIX)
    for c in range(cycles):
        await_send(z2_send.at[early, pl.ds(0, Z - 1), c], EARLY + c)
        await_send(z2_send.at[last, pl.ds(0, Z - 1), c], LAST + c)
        if c == 0:
            await_send(field_recv.at[pl.ds(0, Y - 1)], FIELD)
        else:
            await_send(sum_recv.at[c - 1, pl.ds(0, Y - 1), pl.ds(0, cut)], FIELD + c)
            await_send(sum_recv.at[c - 1, pl.ds(0, Y - 1), pl.ds(cut, size - cut)], FIELD_TAIL + c)
        for at, main in out_pieces(c):
            await_send(out.at[c, pl.ds(0, (Y - 1) * main)], at)

        @pl.when(y == Y - 1)
        def _():
            await_send(out.at[c, pl.ds(0, (Y - 1) * (size - step))], EXTRA + c)

    @pl.when(rank < R - 1)
    def _():
        await_send(halo.at[0], BEFORE)

    @pl.when(rank > 0)
    def _():
        await_send(halo.at[1], AFTER)


def on_device(
    sizes,
    grid,
    basis,
    mix_weight,
    spectral_gain,
    conv_weight,
    lat_offsets,
    lon_offsets,
    ln_gain,
    up_weight,
    down_weight,
):
    X, Z, K, Y = sizes
    cycles, nlon, width = grid.shape
    modes, L, nlat = basis.shape
    C = width * Y
    Q = X * K
    step = nlon // (Y * TILE) * TILE
    size = nlon - (Y - 1) * step
    table = transform_tables(X, Z, K, modes, nlon)
    inverse = np.ascontiguousarray(table.transpose(0, 2, 1))
    perm = np.zeros((nlat, nlat), ml_dtypes.bfloat16)
    perm[np.arange(nlat), cycle_order(X, Z, K, cycles)] = 1
    theta = (math.pi * (np.arange(nlat, dtype=np.float32) + np.float32(0.5)) / nlat).astype(
        np.float32
    )
    quad = (np.float32(math.pi / nlat) * np.sin(theta)).astype(np.float32)[None, :]
    dims = (X, Z, K, Y, cycles, modes, L, nlon, width, step, size)
    any_space = pl.BlockSpec(memory_space=pl.ANY)
    vmem = pl.BlockSpec(memory_space=pltpu.VMEM)
    pad = 8
    n_sem = 5 * modes + 7 * cycles + 4
    around_z = (modes, Z, cycles, 2 * Q, width)
    around_q = (modes, Q, 2, cycles, Z, width)
    scratch = [
        pltpu.VMEM((L,), F32),
        pltpu.VMEM((1, nlat), F32),
        pltpu.VMEM(conv_weight.shape, F32),
        pltpu.SMEM(lat_offsets.shape, jnp.int32),
        pltpu.SMEM(lon_offsets.shape, jnp.int32),
        pltpu.VMEM((1, C), F32),
        pltpu.VMEM((cycles, nlon, width), BF16),
        pltpu.VMEM(table.shape, BF16),
        pltpu.VMEM(inverse.shape, BF16),
        pltpu.VMEM(perm.shape, BF16),
        pltpu.VMEM(basis.shape, F32),
        pltpu.VMEM((Y, 2, C, width), BF16),
        pltpu.VMEM((2 * C, 2 * C), BF16),
        pltpu.VMEM(up_weight.shape, BF16),
        pltpu.VMEM(down_weight.shape, BF16),
        pltpu.VMEM((modes, L, nlat), BF16),
        pltpu.VMEM((modes, nlat, L), BF16),
        pltpu.VMEM(around_z, BF16),
        pltpu.VMEM(around_z, BF16),
        pltpu.VMEM(around_q, BF16),
        pltpu.VMEM(around_q, BF16),
        pltpu.VMEM((modes, Y, X, Z, 2 * width), BF16),
        pltpu.VMEM((modes, Y, X, Z, 2 * width), BF16),
        pltpu.VMEM((modes, X, Y, 2, Z, width), BF16),
        pltpu.VMEM((modes, Q, 2, Z, width), BF16),
        pltpu.VMEM((modes, Q, 2, Z, width), BF16),
        pltpu.VMEM((modes, (cycles - 1) * Q, 2, Z, width), BF16),
        pltpu.VMEM(around_z, BF16),
        pltpu.VMEM(around_z, BF16),
        pltpu.VMEM((2, nlon, width), BF16),
        pltpu.VMEM((cycles + 2, nlon + 2 * pad, width), F32),
        pltpu.VMEM((cycles - 1, nlon, width), F32),
        pltpu.VMEM((nlon, 2 * width), F32),
        pltpu.VMEM((nlon, width), BF16),
        pltpu.VMEM((Y, size, width), BF16),
        pltpu.VMEM((2, nlon, width), BF16),
        pltpu.VMEM((Y, 2, size, width), BF16),
        pltpu.VMEM((cycles - 1, nlon, width), BF16),
        pltpu.VMEM((cycles - 1, Y, size, width), BF16),
        pltpu.VMEM((cycles, Y, size, width), BF16),
        pltpu.SemaphoreType.DMA((2 * cycles + modes + 15,)),
        pltpu.SemaphoreType.DMA((n_sem,)),
        pltpu.SemaphoreType.DMA((n_sem,)),
    ]
    return pl.pallas_call(
        functools.partial(block_kernel, dims),
        out_shape=pltpu.VMEM(grid.shape, BF16),
        in_specs=[any_space] * 14,
        out_specs=vmem,
        scratch_shapes=scratch,
        compiler_params=pltpu.CompilerParams(
            collective_id=0, has_side_effects=True, vmem_limit_bytes=56 * 1024 * 1024
        ),
        name="block",
    )(
        grid,
        jnp.asarray(table),
        jnp.asarray(inverse),
        jnp.asarray(perm),
        basis,
        mix_weight,
        spectral_gain,
        jnp.asarray(quad),
        conv_weight,
        lat_offsets,
        lon_offsets,
        ln_gain.reshape(1, C),
        up_weight,
        down_weight,
    )


def build(finer):
    sizes = tuple(finer.shape[a] for a in (*LAT, "chan"))
    return jax.shard_map(
        functools.partial(on_device, sizes),
        mesh=finer,
        in_specs=(
            P(LAT, None, "chan"),
            P(LAT, None, None),
            P(None, None, "chan"),
            P(),
            P(None, "chan"),
            P(),
            P(),
            P(),
            P(),
            P(),
        ),
        out_specs=P(LAT, None, "chan"),
        check_vma=False,
    )


def solution(mesh):
    return build(
        Mesh(mesh.devices.reshape(4, 16, 2, mesh.shape["chan"]), (*LAT, "chan"))
    )
```
